32 devices in a mesh: ctx: 2 (over x), tp: 4 (over y, core), dp: 4 (over z).
Axes of the slice: x: 2, y: 2, z: 4, core: 2. Of those that a mesh axis runs over, the one named last changes fastest.
Arguments:
- queries: bfloat16 [2048, 3072], P(('dp', 'ctx'), 'tp'), parts along dimension 0, may hold values from -4.5 to 4.5
- key_rows: bfloat16 [2048, 512], P(('dp', 'ctx'), 'tp'), parts along dimension 0, may hold values from -4.5 to 4.5
- value_rows: bfloat16 [2048, 512], P(('dp', 'ctx'), 'tp'), parts along dimension 0, may hold values from -4.5 to 4.5
- residual: bfloat16 [2048, 3072], P(('dp', 'ctx'), 'tp'), parts along dimension 0, may hold values from -9 to 9
- out_weight: bfloat16 [3072, 3072], P('tp')
- attention_gain: float32 [3072], P('tp'), may hold values from 0.25 to 1.75
- middle_gain: float32 [3072], P('tp'), may hold values from 0.25 to 1.75
- output_gain: float32 [3072], P('tp'), may hold values from 0.25 to 1.75
- gate_weight: bfloat16 [4, 3072, 8192], P('tp', None, 'ctx'), may hold values from -0.109375 to 0.109375
- up_weight: bfloat16 [4, 3072, 8192], P('tp', None, 'ctx'), may hold values from -0.109375 to 0.109375
- down_weight: bfloat16 [4, 8192, 3072], P('tp', 'ctx')
- routes: int32 [2048, 2], P(('dp', 'ctx')), parts along dimension 0, may hold values from 0 to 3, all different within a row; in each aligned block of 256 rows (0 to 255, 256 to 511, ...) at most 160 rows name the same one
- gate_shares: float32 [2048, 2], P(('dp', 'ctx')), parts along dimension 0, may hold values from 0 to 1, as said below
Outputs:
- layer_out: bfloat16 [2048, 3072], P(('dp', 'ctx'), 'tp'), parts along dimension 0
The draws below stay inside these ranges and needn't reach their ends.
There are 4 independent parts, one for each index of `dp`. The reference program is written for one: setup_inputs(seed, part) draws one part's arguments, and reference() takes and returns one part's arrays. A program takes and returns all parts, laid end to end along the dimension named above; an argument that names none is the same for every part. Nothing has to cross between parts.
Inputs may be any that keep to these rules, and one draw needn't show every extreme that they name: `routes`: within each block of 256 consecutive tokens each expert is named by at most 160 tokens, a bound that some block reaches; a token's 2 experts differ. `gate_shares`: each token's weights are positive and sum to one.
All inputs are finite; a program needn't handle non-finite values.
Results may differ from the reference program's by a relative error of at most 0.0067.
Values may be sent and summed in bfloat16 or wider, within the bound.
A program may use at most 192 MiB of HBM per device.

```python
import math
import jax
import jax.numpy as jnp
import numpy as np
from jax import lax

D = 3072
HEADS = 24
KVH = 4
HD = 128
FF = 8192
EXPERTS = 4
TOP = 2
TOK_DEV = 256
CAP = 160
TOKENS = 512
FF_PART = 4096
N_CTX = 2


def column_scale(key, width, steep):
    fraction = jnp.arange(width, dtype=jnp.float32) / width
    jitter = jnp.exp(jax.random.uniform(key, (width,), jnp.float32, math.log(0.7), math.log(1.4)))
    return steep ** fraction * jitter


def rough_field(key, shape):
    return jnp.clip(jax.random.normal(key, shape, jnp.float32), -4.0, 4.0)


def draw_residual(key, part):
    base = rough_field(jax.random.fold_in(key, 1), (TOKENS, D))
    steep = 3.0
    return (0.4 * base * column_scale(jax.random.fold_in(key, 2), D, steep)[None, :]).astype(jnp.bfloat16)


def draw_out_weight(key, part):
    fan_rows = HEADS * HD
    base = rough_field(jax.random.fold_in(key, 1), (fan_rows, D)) / math.sqrt(fan_rows)
    steep = 3.0
    return (base * column_scale(jax.random.fold_in(key, 2), D, steep)[None, :]).astype(jnp.bfloat16)


def draw_down_weight(key, part):
    base = rough_field(jax.random.fold_in(key, 1), (EXPERTS, FF, D)) / math.sqrt(FF)
    steep = 3.0
    return (base * column_scale(jax.random.fold_in(key, 2), D, steep)[None, None, :]).astype(jnp.bfloat16)


def draw_queries(key, part):
    base = jnp.clip(jax.random.normal(jax.random.fold_in(key, 1), (TOKENS, HEADS, HD), jnp.float32), -4.5, 4.5)
    return base.reshape(TOKENS, HEADS * HD).astype(jnp.bfloat16)


def draw_key_rows(key, part):
    base = jnp.clip(jax.random.normal(jax.random.fold_in(key, 2), (TOKENS, KVH, HD), jnp.float32), -4.5, 4.5)
    return base.reshape(TOKENS, KVH * HD).astype(jnp.bfloat16)


def draw_gate_shares(key, part):
    share = jax.random.uniform(jax.random.fold_in(key, 1), (TOKENS,), jnp.float32, 0.1, 0.9)
    return jnp.stack([share, 1.0 - share], axis=1)


def levels(rng, shape, pieces, smallest, top_value):
    factor_of, own = 1.0, jax.random.fold_in(rng, 6)
    for position, shards_of in pieces:
        heights = jnp.exp(jax.random.uniform(jax.random.fold_in(own, position), (shards_of,), jnp.float32, smallest / len(pieces), top_value / len(pieces)))
        factor_of = factor_of * jnp.repeat(heights, shape[position] // shards_of).reshape([-1 if axis == position else 1 for axis in range(len(shape))])
    return factor_of


def deal_out(own_key, own, number, rows, number_of, top, reach, slope):
    order = jax.random.permutation(own_key, number_of)
    heavy_load, ordinary = portions_of(number_of, rows * top, reach, slope, True), portions_of(number_of, rows * top, reach, slope, False)
    places = jnp.arange(number_of)

    def named(tallies, turn):
        used = int((tallies > 0).sum())
        fixed = max(1, used // 4)
        moved = fixed + (places - fixed + turn * (used - fixed)) % max(1, number_of - fixed)
        return jnp.zeros((number_of,), jnp.int32).at[order[jnp.where(places < fixed, places, moved)]].set(jnp.asarray(tallies, jnp.int32))

    tallies = jnp.where(number % 4 == 0, named(heavy_load, number // 4), named(ordinary, number - number // 4 - 1))
    mixed = jax.random.permutation(jax.random.fold_in(own, 3), number_of)
    source_of, taker = mixed[0:number_of // 2 * 2:2], mixed[1:number_of // 2 * 2:2]
    slack = jnp.minimum(tallies[source_of] - 1, reach - tallies[taker]) // 2
    slack = jnp.where((source_of == order[0]) | (taker == order[0]) | (tallies[taker] == 0), 0, jnp.maximum(slack, 0))
    moved = jax.random.randint(jax.random.fold_in(own, 4), (number_of // 2,), 0, 1 << 20) % (slack + 1)
    tallies = tallies.at[source_of].add(-moved).at[taker].add(moved)
    items = jnp.searchsorted(jnp.cumsum(tallies), jnp.arange(rows * top), side="right").astype(jnp.int32)
    listing = items.reshape(top, rows).T
    listing = listing[jax.random.permutation(jax.random.fold_in(own, 1), rows)]
    turn = jax.random.randint(jax.random.fold_in(own, 2), (rows, 1), 0, top)
    return jnp.take_along_axis(listing, (jnp.arange(top)[None, :] + turn) % top, axis=1)


def portions_of(number_of, total, reach, skew, full):
    weights = [(1 << 20) // math.isqrt(standing ** skew) + 1 for standing in range(1, number_of + 1)]
    largest = reach if full else min(reach, max(-(-total // number_of), total * weights[0] // sum(weights)))
    least = 1 if total - largest >= number_of - 1 else 0
    holding, spare = [largest] + [least] * (number_of - 1), total - largest - least * (number_of - 1)
    while spare > 0:
        movable = [i for i in range(1, number_of) if holding[i] < largest] or [i for i in range(1, number_of) if holding[i] < reach]
        pool, budget = sum([weights[i] for i in movable]), spare
        for i in movable:
            more = min(reach - holding[i], max(1, budget * weights[i] // pool), spare)
            holding[i] = holding[i] + more
            spare = spare - more
    return np.array(holding)


def bell_draw(key, shape, deviation, limit, split=(), held_as=jnp.bfloat16):
    array = deviation * jax.random.normal(key, shape, jnp.float32)
    if split:
        array = array * levels(key, shape, split, -0.22, 0.18)
    return jnp.clip(array, -limit, limit).astype(held_as)


def setup_inputs(seed: int = 0, part: int = 0) -> dict:
    arg_keys = jax.random.split(jax.random.key(seed), 14)
    part_splits = jax.random.split(jax.random.fold_in(arg_keys[13], part), 14)
    queries = draw_queries(jax.random.fold_in(jax.random.fold_in(arg_keys[13], part), 71), part)
    key_rows = draw_key_rows(jax.random.fold_in(jax.random.fold_in(arg_keys[13], part), 71), part)
    value_rows = bell_draw(part_splits[2], (TOKENS, KVH * HD), 1.0, 4.5, ((0, 2), (1, 4)))
    residual = draw_residual(jax.random.fold_in(jax.random.fold_in(arg_keys[13], part), 71), part)
    out_weight = draw_out_weight(jax.random.fold_in(arg_keys[13], 71), part)
    attention_gain = jnp.clip(1.0 + 0.15 * jax.random.normal(arg_keys[5], (D,), jnp.float32), 0.25, 1.75)
    middle_gain = jnp.clip(1.0 + 0.15 * jax.random.normal(arg_keys[6], (D,), jnp.float32), 0.25, 1.75)
    output_gain = jnp.clip(1.0 + 0.15 * jax.random.normal(arg_keys[7], (D,), jnp.float32), 0.25, 1.75)
    gate_weight = bell_draw(arg_keys[8], (EXPERTS, D, FF), D ** -0.5, 0.109375, ((0, 4), (2, 2)))
    up_weight = bell_draw(arg_keys[9], (EXPERTS, D, FF), D ** -0.5, 0.109375, ((0, 4), (2, 2)))
    down_weight = draw_down_weight(jax.random.fold_in(arg_keys[13], 71), part)
    routes_keys = jax.random.split(jax.random.fold_in(part_splits[11], 1), TOKENS // TOK_DEV)
    routes_turns = jax.random.permutation(jax.random.fold_in(part_splits[11], 3), TOKENS // TOK_DEV)
    routes = jax.vmap(lambda own, number: deal_out(jax.random.fold_in(part_splits[11], 2), own, number, TOK_DEV, EXPERTS, TOP, CAP, 1))(routes_keys, routes_turns).reshape((TOKENS, TOP))
    gate_shares = draw_gate_shares(jax.random.fold_in(jax.random.fold_in(arg_keys[13], part), 71), part)
    return {"queries": queries, "key_rows": key_rows, "value_rows": value_rows, "residual": residual, "out_weight": out_weight, "attention_gain": attention_gain, "middle_gain": middle_gain, "output_gain": output_gain, "gate_weight": gate_weight, "up_weight": up_weight, "down_weight": down_weight, "routes": routes, "gate_shares": gate_shares}


epsilon = 1e-06
masked_score = -1e+30

def reference(queries, key_rows, value_rows, residual, out_weight, attention_gain, middle_gain, output_gain, gate_weight, up_weight, down_weight, routes, gate_shares):
    group_size = HEADS // KVH
    scaling = 1.0 / math.sqrt(HD)
    positions = jnp.arange(TOKENS, dtype=jnp.int32)
    causal = positions[None, :] <= positions[:, None]
    query_heads = queries.reshape(TOKENS, HEADS, HD).transpose(1, 0, 2)
    key_heads = key_rows.reshape(TOKENS, KVH, HD).transpose(1, 0, 2)
    value_heads = value_rows.reshape(TOKENS, KVH, HD).transpose(1, 0, 2)

    def one_head(head_index):
        query_block = query_heads[head_index]
        key_block = key_heads[head_index // group_size]
        value_block = value_heads[head_index // group_size]
        scores = jnp.dot(query_block, key_block.T, preferred_element_type=jnp.float32) * scaling
        scores = jnp.where(causal, scores, jnp.float32(masked_score))
        weights = jnp.exp(scores - lax.optimization_barrier(jnp.max(scores, axis=1, keepdims=True)))
        row_sum = lax.optimization_barrier(jnp.sum(weights, axis=1, keepdims=True))
        return jnp.dot(weights.astype(jnp.bfloat16), value_block, preferred_element_type=jnp.float32) / row_sum
    attended = lax.map(one_head, jnp.arange(HEADS, dtype=jnp.int32))
    attended = attended.transpose(1, 0, 2).reshape(TOKENS, HEADS * HD).astype(jnp.bfloat16)
    projected = jnp.dot(attended, out_weight, preferred_element_type=jnp.float32)
    middle = residual.astype(jnp.float32) + attention_gain * projected * lax.rsqrt(lax.optimization_barrier(jnp.sum(projected * projected, axis=1, keepdims=True)) / D + epsilon)
    expert_in = (middle_gain * middle * lax.rsqrt(lax.optimization_barrier(jnp.sum(middle * middle, axis=1, keepdims=True)) / D + epsilon)).astype(jnp.bfloat16)
    blocks = TOKENS // TOK_DEV
    chosen = routes.reshape(blocks, TOK_DEV * TOP)
    onehot = (chosen[:, :, None] == jnp.arange(EXPERTS, dtype=jnp.int32)[None, None, :]).astype(jnp.int32)
    before = jnp.cumsum(onehot, axis=1) - onehot
    slot_index = lax.optimization_barrier(jnp.sum(before * onehot, axis=2)).reshape(-1)
    block_of = jnp.arange(TOKENS * TOP, dtype=jnp.int32) // (TOK_DEV * TOP)
    row_of = (block_of * CAP + slot_index).astype(jnp.int32)
    flat_ids = routes.reshape(-1)
    source_rows = jnp.repeat(expert_in, TOP, axis=0)

    def one_expert(expert):
        target = jnp.where(flat_ids == expert, row_of, blocks * CAP).astype(jnp.int32)
        buffer = jnp.zeros((blocks * CAP, D), jnp.bfloat16).at[target].set(source_rows, mode='drop')
        gate_all = gate_weight[expert]
        up_all = up_weight[expert]
        down_all = down_weight[expert]
        running = jnp.zeros((blocks * CAP, D), jnp.float32)
        for section in range(N_CTX):
            first_unit = section * FF_PART
            gate_part = jnp.dot(buffer, gate_all[:, first_unit:first_unit + FF_PART], preferred_element_type=jnp.float32)
            up_part = jnp.dot(buffer, up_all[:, first_unit:first_unit + FF_PART], preferred_element_type=jnp.float32)
            hidden = (jax.nn.silu(gate_part) * up_part).astype(jnp.bfloat16)
            portion = jnp.dot(hidden, down_all[first_unit:first_unit + FF_PART], preferred_element_type=jnp.float32).astype(jnp.bfloat16)
            running = running + portion.astype(jnp.float32)
        return running.astype(jnp.bfloat16)
    expert_out = lax.map(one_expert, jnp.arange(EXPERTS, dtype=jnp.int32))
    picked = expert_out[flat_ids, row_of].astype(jnp.float32).reshape(TOKENS, TOP, D)
    mixture = gate_shares[:, 0:1] * picked[:, 0]
    for choice_slot in range(1, TOP):
        mixture = mixture + gate_shares[:, choice_slot:choice_slot + 1] * picked[:, choice_slot]
    normed = output_gain * mixture * lax.rsqrt(lax.optimization_barrier(jnp.sum(mixture * mixture, axis=1, keepdims=True)) / D + epsilon)
    return (middle + normed).astype(jnp.bfloat16)
```

```python
import functools
import math

import jax
import jax.numpy as jnp
from jax import lax
from jax.experimental import pallas as pl
from jax.experimental.pallas import tpu as pltpu
from jax.sharding import PartitionSpec as P

D = 3072
HD = 128
TP = 4
CAP = 160

epsilon = 1e-06
masked_score = -1e30
VMEM_LIMIT = 60 << 20
f32 = jnp.float32
bf16 = jnp.bfloat16


def peers(n):
    c = lax.axis_index("ctx")
    t = lax.axis_index("tp")
    sib = t + 1 - 2 * (t % 2)
    far = (t + 2) % TP
    diag = TP - 1 - t
    others = [(c + d) % n for d in range(1, n)]
    return c, t, sib, far, diag, others


def remote(src, dst, send_sem, recv_sem, **where):
    return pltpu.make_async_remote_copy(
        src_ref=src,
        dst_ref=dst,
        send_sem=send_sem,
        recv_sem=recv_sem,
        device_id=where,
        device_id_type=pl.DeviceIdType.MESH,
    )


def enter(n, tp_peers, others):
    barrier = pltpu.get_barrier_semaphore()
    for p in tp_peers:
        pl.semaphore_signal(barrier, inc=1, device_id={"tp": p}, device_id_type=pl.DeviceIdType.MESH)
    for o in others:
        pl.semaphore_signal(barrier, inc=1, device_id={"ctx": o}, device_id_type=pl.DeviceIdType.MESH)
    pl.semaphore_wait(barrier, len(tp_peers) + len(others))


def columns_to_rows(columns, tokens):
    lane = lax.broadcasted_iota(jnp.int32, (tokens, 128), 1)
    packed = jnp.zeros((tokens, 128), f32)
    for i, column in enumerate(columns):
        packed = jnp.where(lane == i, column, packed)
    return packed.T[:8]


def rows_to_columns(rows):
    return jnp.concatenate([rows, jnp.zeros((120, rows.shape[1]), f32)], axis=0).T


def front_kernel(
    n,
    q_ref,
    k_ref,
    v_ref,
    res_ref,
    ow_hbm,
    ag_ref,
    mg_ref,
    info_ref,
    rows_ref,
    mid_ref,
    all_info,
    k_all,
    v_all,
    ow,
    att,
    part_send,
    part_recv,
    far_send,
    far_recv,
    stat_recv,
    tok,
    ow_sem,
    kv_send,
    kv_recv,
    part_ss,
    part_rs,
    far_sem,
    stat_ss,
    stat_rs,
    tok_ss,
    tok_rs,
):
    tokens, width = q_ref.shape
    half_rows = tokens // 2
    c, t, sib, far, diag, others = peers(n)
    weight_copy = pltpu.make_async_copy(ow_hbm, ow, ow_sem)
    weight_copy.start()
    enter(n, (sib, far, diag), others)

    k_all[c] = k_ref[...]
    v_all[c] = v_ref[...]
    before = (
        lax.broadcasted_iota(jnp.int32, (tokens, tokens), 0)
        < lax.broadcasted_iota(jnp.int32, (tokens, tokens), 1)
    ).astype(f32).astype(bf16)
    info = info_ref[...]
    slots = jnp.dot(info.astype(bf16), before, preferred_element_type=f32)
    slots = jnp.where(info > 0.5, slots, -1.0)
    row = lax.broadcasted_iota(jnp.int32, info.shape, 0)
    all_info[c] = jnp.where(row == 0, slots, info)
    kv_copies = []
    for i, o in enumerate(others):
        for j, ref in enumerate((k_all, v_all, all_info)):
            copy = remote(ref.at[c], ref.at[c], kv_send.at[i, j], kv_recv.at[c, j], ctx=o)
            copy.start()
            kv_copies.append(copy)
    for o in others:
        for j, ref in enumerate((k_all, v_all, all_info)):
            remote(ref.at[o], ref.at[o], kv_send.at[0, j], kv_recv.at[o, j], ctx=o).wait_recv()

    keys = k_all[...].reshape(n * tokens, HD)
    values = v_all[...].reshape(n * tokens, HD)
    allowed = lax.broadcasted_iota(
        jnp.int32, (tokens, n * tokens), 1
    ) <= c * tokens + lax.broadcasted_iota(jnp.int32, (tokens, n * tokens), 0)
    for h in range(width // HD):
        scores = lax.dot_general(
            q_ref[:, h * HD : (h + 1) * HD],
            keys,
            (((1,), (1,)), ((), ())),
            preferred_element_type=f32,
        ) * (1.0 / math.sqrt(HD))
        scores = jnp.where(allowed, scores, masked_score)
        weights = jnp.exp(scores - jnp.max(scores, axis=1, keepdims=True))
        total = jnp.sum(weights, axis=1, keepdims=True)
        weighted = jnp.dot(weights.astype(bf16), values, preferred_element_type=f32)
        att[:, h * HD : (h + 1) * HD] = (weighted / total).astype(bf16)

    weight_copy.wait()

    def partial(block):
        cols = pl.ds(pl.multiple_of(block * width, 128), width)
        return jnp.dot(att[...], ow[:, cols], preferred_element_type=f32)

    sib_copies = []
    for j, block in enumerate((diag, sib)):
        part_send[j] = partial(block).astype(bf16)
        copy = remote(
            part_send.at[j], part_recv.at[j], part_ss.at[j], part_rs.at[j], tp=sib
        )
        copy.start()
        sib_copies.append(copy)
    keep = partial(far)
    sib_copies[0].wait()
    far_send[...] = (keep + part_recv[0].astype(f32)).astype(bf16)
    far_copy = remote(far_send, far_recv, far_sem.at[0], far_sem.at[1], tp=far)
    far_copy.start()
    own = partial(t)
    sib_copies[1].wait()
    own = own + part_recv[1].astype(f32)
    far_copy.wait()
    own = own + far_recv[...].astype(f32)

    residual = res_ref[...].astype(f32)
    gained = ag_ref[...] * own
    stat_recv[t] = columns_to_rows(
        [
            jnp.sum(own * own, axis=1, keepdims=True),
            jnp.sum(residual * residual, axis=1, keepdims=True),
            jnp.sum(residual * gained, axis=1, keepdims=True),
            jnp.sum(gained * gained, axis=1, keepdims=True),
        ],
        tokens,
    )
    stat_copies = []
    for i, p in enumerate((far, diag, sib)):
        copy = remote(stat_recv.at[t], stat_recv.at[t], stat_ss.at[i], stat_rs.at[t], tp=p)
        copy.start()
        stat_copies.append(copy)
    for i, p in enumerate((far, diag, sib)):
        remote(stat_recv.at[p], stat_recv.at[p], stat_ss.at[i], stat_rs.at[p], tp=p).wait_recv()
    sums = rows_to_columns(stat_recv[0] + stat_recv[1] + stat_recv[2] + stat_recv[3])
    scale = lax.rsqrt(sums[:, 0:1] / D + epsilon)
    squares = sums[:, 1:2] + 2.0 * scale * sums[:, 2:3] + scale * scale * sums[:, 3:4]
    middle = residual + gained * scale
    mid_ref[...] = middle
    tok[c, t] = (
        mg_ref[...] * middle * lax.rsqrt(jnp.maximum(squares, 0.0) / D + epsilon)
    ).astype(bf16)

    sent = []

    def piece(cb, tb, half):
        return tok.at[cb, tb, pl.ds(half * half_rows, half_rows)]

    def push(cb, tb, half, **where):
        ref = piece(cb, tb, half)
        copy = remote(ref, ref, tok_ss.at[len(sent)], tok_rs.at[cb, tb, half], **where)
        copy.start()
        sent.append(copy)

    def arrive(cb, tb, half):
        ref = piece(cb, tb, half)
        remote(ref, ref, tok_ss.at[0], tok_rs.at[cb, tb, half], tp=sib).wait_recv()

    for half in (0, 1):
        for o in others:
            push(c, t, half, ctx=o)
        push(c, t, 1 - half, tp=far)
    for half in (0, 1):
        push(c, t, half, tp=sib)
    for o in others:
        arrive(o, t, 0)
        push(o, t, 0, tp=far)
        push(o, t, 0, tp=sib)
    arrive(c, far, 1)
    for o in others:
        push(c, far, 1, ctx=o)
    push(c, far, 1, tp=sib)
    for o in others:
        arrive(o, t, 1)
        push(o, t, 1, tp=sib)
    arrive(c, far, 0)
    push(c, far, 0, tp=sib)
    for o in others:
        for half in (0, 1):
            arrive(o, far, half)
            push(o, far, half, tp=sib)
    for b in [c] + others:
        for block in (sib, diag):
            for half in (0, 1):
                arrive(b, block, half)
    for b in range(n):
        table = (
            lax.broadcasted_iota(jnp.int32, (CAP, tokens), 0).astype(f32) == all_info[b, 0:1, :]
        ).astype(f32).astype(bf16)
        for block in range(TP):
            rows_ref[b, :, block * width : (block + 1) * width] = jnp.dot(
                table, tok[b, block], preferred_element_type=f32
            ).astype(bf16)
    for copy in kv_copies + stat_copies + sent:
        copy.wait_send()


def front(n, queries, key_rows, value_rows, residual, out_weight, ag, mg, info):
    tokens, width = queries.shape
    vmem = pl.BlockSpec(memory_space=pltpu.VMEM)
    dma = pltpu.SemaphoreType.DMA
    pushes = 2 * (n - 1) + 2 + 2 + 2 * (n - 1) + (n - 1) + 1 + (n - 1) + 1 + 2 * (n - 1)
    return pl.pallas_call(
        functools.partial(front_kernel, n),
        out_shape=(
            jax.ShapeDtypeStruct((n, CAP, D), bf16),
            jax.ShapeDtypeStruct((tokens, width), f32),
            jax.ShapeDtypeStruct((n, 8, tokens), f32),
        ),
        in_specs=[vmem] * 4 + [pl.BlockSpec(memory_space=pl.ANY)] + [vmem] * 3,
        out_specs=(vmem, vmem, vmem),
        scratch_shapes=[
            pltpu.VMEM((n, tokens, HD), bf16),
            pltpu.VMEM((n, tokens, HD), bf16),
            pltpu.VMEM(out_weight.shape, bf16),
            pltpu.VMEM((tokens, width), bf16),
            pltpu.VMEM((2, tokens, width), bf16),
            pltpu.VMEM((2, tokens, width), bf16),
            pltpu.VMEM((tokens, width), bf16),
            pltpu.VMEM((tokens, width), bf16),
            pltpu.VMEM((TP, 8, tokens), f32),
            pltpu.VMEM((n, TP, tokens, width), bf16),
            dma,
            dma((max(n - 1, 1), 3)),
            dma((n, 3)),
            dma((2,)),
            dma((2,)),
            dma((2,)),
            dma((3,)),
            dma((TP,)),
            dma((pushes,)),
            dma((n, TP, 2)),
        ],
        compiler_params=pltpu.CompilerParams(
            collective_id=0, has_side_effects=True, vmem_limit_bytes=VMEM_LIMIT
        ),
        name="front",
    )(queries, key_rows, value_rows, residual, out_weight, ag, mg, info)


def expert_kernel(steps, tile, n, x_ref, info_ref, gate_ref, up_ref, down_ref, out_ref, hidden, row_gate):
    step = pl.program_id(0)

    @pl.when(step == 0)
    def _():
        tokens = info_ref.shape[2]
        for b in range(n):
            chosen = (
                lax.broadcasted_iota(jnp.int32, (CAP, tokens), 0).astype(f32)
                == info_ref[b, 0:1, :]
            )
            row_gate[b * CAP : (b + 1) * CAP, :] = jnp.sum(
                jnp.where(chosen, info_ref[b, 1:2, :], 0.0), axis=1, keepdims=True
            )

    @pl.when(step < steps)
    def _():
        gate_part = jnp.dot(x_ref[...], gate_ref[0], preferred_element_type=f32)
        up_part = jnp.dot(x_ref[...], up_ref[0], preferred_element_type=f32)
        hidden[:, pl.ds(pl.multiple_of(step * tile, 128), tile)] = (
            gate_part / (1.0 + jnp.exp(-gate_part)) * up_part
        ).astype(bf16)

    @pl.when(step >= steps)
    def _():
        out_ref[...] = (
            jnp.dot(hidden[...], down_ref[0], preferred_element_type=f32) * row_gate[...]
        ).astype(bf16)


def experts(n, rows, info, gate_weight, up_weight, down_weight):
    m = rows.shape[0]
    units = gate_weight.shape[2]
    tile, out_tile = 512, 384
    steps = units // tile
    out_steps = D // out_tile

    def early(i):
        return (0, 0, jnp.minimum(i, steps - 1))

    return pl.pallas_call(
        functools.partial(expert_kernel, steps, tile, n),
        grid=(steps + out_steps,),
        out_shape=jax.ShapeDtypeStruct((m, D), bf16),
        in_specs=[
            pl.BlockSpec((m, D), lambda i: (0, 0), pipeline_mode=pl.Buffered(1)),
            pl.BlockSpec(info.shape, lambda i: (0, 0, 0)),
            pl.BlockSpec((1, D, tile), early),
            pl.BlockSpec((1, D, tile), early),
            pl.BlockSpec((1, units, out_tile), lambda i: (0, 0, jnp.maximum(i - steps, 0))),
        ],
        out_specs=pl.BlockSpec((m, out_tile), lambda i: (0, jnp.maximum(i - steps, 0))),
        scratch_shapes=[pltpu.VMEM((m, units), bf16), pltpu.VMEM((m, 1), f32)],
        compiler_params=pltpu.CompilerParams(
            dimension_semantics=("arbitrary",), vmem_limit_bytes=VMEM_LIMIT
        ),
        name="experts",
    )(rows, info, gate_weight, up_weight, down_weight)


def back_kernel(
    n,
    por_ref,
    info_ref,
    mid_ref,
    og_ref,
    out_ref,
    one_send,
    one_recv,
    sums,
    two_send,
    turn_far,
    turn_ctx,
    from_far,
    from_ctx,
    stat_recv,
    one_ss,
    one_rs,
    two_ss,
    turn_far_rs,
    turn_ctx_rs,
    from_far_rs,
    from_ctx_rs,
    stat_ss,
    stat_rs,
):
    tokens, width = mid_ref.shape
    half_rows = tokens // 2
    first, second = pl.ds(0, half_rows), pl.ds(half_rows, half_rows)
    c, t, sib, far, diag, others = peers(n)
    enter(n, (sib, far, diag), others)

    def spread(b):
        slot = rows_to_columns(info_ref[b])[:, 0:1]
        return (
            lax.broadcasted_iota(jnp.int32, (tokens, CAP), 1).astype(f32) == slot
        ).astype(f32).astype(bf16)

    def partial(table, b, block):
        cols = pl.ds(pl.multiple_of(block * width, 128), width)
        return jnp.dot(table, por_ref[b, :, cols], preferred_element_type=f32)

    copies = []

    def push(src, dst, ss, rs, **where):
        copy = remote(src, dst, ss, rs, **where)
        copy.start()
        copies.append(copy)

    order = others + [c]
    tables = [spread(b) for b in order]
    for j, block in ((1, diag), (0, sib)):
        for i, b in enumerate(order):
            one_send[b, j] = partial(tables[i], b, block).astype(bf16)
            push(one_send.at[b, j], one_recv.at[b, j], one_ss.at[i, j], one_rs.at[b, j], tp=sib)
    for j, block in ((1, far), (0, t)):
        for i, b in enumerate(order):
            own = partial(tables[i], b, block)
            remote(
                one_send.at[b, j], one_recv.at[b, j], one_ss.at[i, j], one_rs.at[b, j], tp=sib
            ).wait_recv()
            own = own + one_recv[b, j].astype(f32)
            sums[b, j] = own
            if i < n - 1:
                two_send[b, j] = own.astype(bf16)
                if j == 1:
                    push(
                        two_send.at[b, 1, first],
                        turn_far.at[b],
                        two_ss.at[i, 0],
                        turn_far_rs.at[b],
                        tp=far,
                    )
                    push(
                        two_send.at[b, 1, second],
                        turn_ctx.at[c],
                        two_ss.at[i, 1],
                        turn_ctx_rs.at[c],
                        ctx=b,
                    )
                else:
                    push(
                        two_send.at[b, 0, second],
                        from_ctx.at[c, second],
                        two_ss.at[i, 2],
                        from_ctx_rs.at[c, 1],
                        ctx=b,
                    )
            elif j == 1:
                two_send[c, 1, first] = own[:half_rows].astype(bf16)
                push(
                    two_send.at[c, 1, first],
                    from_far.at[first],
                    two_ss.at[i, 0],
                    from_far_rs.at[0],
                    tp=far,
                )
    for i, b in enumerate(others):
        remote(
            two_send.at[b, 1, first], turn_far.at[b], two_ss.at[i, 0], turn_far_rs.at[b], tp=far
        ).wait_recv()
        two_send[b, 0, first] = (sums[b, 0, first] + turn_far[b].astype(f32)).astype(bf16)
        push(
            two_send.at[b, 0, first],
            from_ctx.at[c, first],
            two_ss.at[i, 3],
            from_ctx_rs.at[c, 0],
            ctx=b,
        )
    turned = sums[c, 1, second]
    for i, b in enumerate(others):
        remote(
            two_send.at[b, 1, second], turn_ctx.at[b], two_ss.at[i, 1], turn_ctx_rs.at[b], ctx=b
        ).wait_recv()
        turned = turned + turn_ctx[b].astype(f32)
    two_send[c, 1, second] = turned.astype(bf16)
    push(
        two_send.at[c, 1, second],
        from_far.at[second],
        two_ss.at[n - 1, 1],
        from_far_rs.at[1],
        tp=far,
    )
    mixture = sums[c, 0]
    for b in others:
        for half, rows in ((1, second), (0, first)):
            remote(
                two_send.at[b, 0, rows],
                from_ctx.at[b, rows],
                two_ss.at[0, 2],
                from_ctx_rs.at[b, half],
                ctx=b,
            ).wait_recv()
        mixture = mixture + from_ctx[b].astype(f32)
    for half, rows in ((0, first), (1, second)):
        remote(
            two_send.at[c, 1, rows],
            from_far.at[rows],
            two_ss.at[0, 0],
            from_far_rs.at[half],
            tp=far,
        ).wait_recv()
    mixture = mixture + from_far[...].astype(f32)

    stat_recv[t] = columns_to_rows(
        [jnp.sum(mixture * mixture, axis=1, keepdims=True)], tokens
    )
    for i, p in enumerate((far, diag, sib)):
        push(stat_recv.at[t], stat_recv.at[t], stat_ss.at[i], stat_rs.at[t], tp=p)
    for i, p in enumerate((far, diag, sib)):
        remote(stat_recv.at[p], stat_recv.at[p], stat_ss.at[i], stat_rs.at[p], tp=p).wait_recv()
    squares = rows_to_columns(stat_recv[0] + stat_recv[1] + stat_recv[2] + stat_recv[3])[:, 0:1]
    normed = og_ref[...] * mixture * lax.rsqrt(squares / D + epsilon)
    out_ref[...] = (mid_ref[...] + normed).astype(bf16)
    for copy in copies:
        copy.wait_send()


def back(n, portions, info, middle, og):
    tokens, width = middle.shape
    vmem = pl.BlockSpec(memory_space=pltpu.VMEM)
    dma = pltpu.SemaphoreType.DMA
    return pl.pallas_call(
        functools.partial(back_kernel, n),
        out_shape=jax.ShapeDtypeStruct((tokens, width), bf16),
        in_specs=[vmem] * 4,
        out_specs=vmem,
        scratch_shapes=[
            pltpu.VMEM((n, 2, tokens, width), bf16),
            pltpu.VMEM((n, 2, tokens, width), bf16),
            pltpu.VMEM((n, 2, tokens, width), f32),
            pltpu.VMEM((n, 2, tokens, width), bf16),
            pltpu.VMEM((n, tokens // 2, width), bf16),
            pltpu.VMEM((n, tokens // 2, width), bf16),
            pltpu.VMEM((tokens, width), bf16),
            pltpu.VMEM((n, tokens, width), bf16),
            pltpu.VMEM((TP, 8, tokens), f32),
            dma((n, 2)),
            dma((n, 2)),
            dma((n, 4)),
            dma((n,)),
            dma((n,)),
            dma((2,)),
            dma((n, 2)),
            dma((3,)),
            dma((TP,)),
        ],
        compiler_params=pltpu.CompilerParams(
            collective_id=1, has_side_effects=True, vmem_limit_bytes=VMEM_LIMIT
        ),
        name="back",
    )(portions, info, middle, og)


def shards(
    n,
    queries,
    key_rows,
    value_rows,
    residual,
    out_weight,
    attention_gain,
    middle_gain,
    output_gain,
    gate_weight,
    up_weight,
    down_weight,
    routes,
    gate_shares,
):
    tokens = queries.shape[0]
    mine = routes == lax.axis_index("tp")
    named = jnp.sum(mine.astype(f32), axis=1)
    gate = jnp.sum(jnp.where(mine, gate_shares, 0.0), axis=1)
    row = jnp.arange(8, dtype=jnp.int32)[:, None]
    info = jnp.where(row == 0, named[None, :], jnp.where(row == 1, gate[None, :], 0.0))
    rows, middle, info = front(
        n,
        queries,
        key_rows,
        value_rows,
        residual,
        out_weight,
        attention_gain[None, :],
        middle_gain[None, :],
        info,
    )
    portions = experts(
        n, rows.reshape(n * CAP, D), info, gate_weight, up_weight, down_weight
    )
    return back(n, portions.reshape(n, CAP, D), info, middle, output_gain[None, :])


def solution(mesh):
    in_specs = (
        P(("dp", "ctx"), "tp"),
        P(("dp", "ctx"), "tp"),
        P(("dp", "ctx"), "tp"),
        P(("dp", "ctx"), "tp"),
        P("tp", None),
        P("tp"),
        P("tp"),
        P("tp"),
        P("tp", None, "ctx"),
        P("tp", None, "ctx"),
        P("tp", "ctx", None),
        P(("dp", "ctx"), None),
        P(("dp", "ctx"), None),
    )
    out_specs = P(("dp", "ctx"), "tp")
    return jax.shard_map(
        functools.partial(shards, mesh.shape["ctx"]),
        mesh=mesh,
        in_specs=in_specs,
        out_specs=out_specs,
        check_vma=False,
    )
```

```python
import functools
import math

import jax
import jax.numpy as jnp
from jax import lax
from jax.experimental import pallas as pl
from jax.experimental.pallas import tpu as pltpu
from jax.sharding import PartitionSpec as P

D = 3072
HD = 128
TP = 4
CAP = 160

epsilon = 1e-06
masked_score = -1e30
VMEM_LIMIT = 62 << 20
OUT_TILE = 384
f32 = jnp.float32
bf16 = jnp.bfloat16


def peers(n):
    c = lax.axis_index("ctx")
    t = lax.axis_index("tp")
    sib = t + 1 - 2 * (t % 2)
    far = (t + 2) % TP
    diag = TP - 1 - t
    others = [(c + d) % n for d in range(1, n)]
    return c, t, sib, far, diag, others


def remote(src, dst, send_sem, recv_sem, **where):
    return pltpu.make_async_remote_copy(
        src_ref=src,
        dst_ref=dst,
        send_sem=send_sem,
        recv_sem=recv_sem,
        device_id=where,
        device_id_type=pl.DeviceIdType.MESH,
    )


def enter(n, tp_peers, others):
    barrier = pltpu.get_barrier_semaphore()
    for p in tp_peers:
        pl.semaphore_signal(barrier, inc=1, device_id={"tp": p}, device_id_type=pl.DeviceIdType.MESH)
    for o in others:
        pl.semaphore_signal(barrier, inc=1, device_id={"ctx": o}, device_id_type=pl.DeviceIdType.MESH)
    pl.semaphore_wait(barrier, len(tp_peers) + len(others))


def columns_to_rows(columns, tokens):
    lane = lax.broadcasted_iota(jnp.int32, (tokens, 128), 1)
    packed = jnp.zeros((tokens, 128), f32)
    for i, column in enumerate(columns):
        packed = jnp.where(lane == i, column, packed)
    return packed.T[:8]


def rows_to_columns(rows):
    return jnp.concatenate([rows, jnp.zeros((120, rows.shape[1]), f32)], axis=0).T


def front_kernel(
    n,
    q_ref,
    k_ref,
    v_ref,
    res_ref,
    ow_hbm,
    ag_ref,
    mg_ref,
    info_ref,
    gate_hbm,
    up_hbm,
    down_hbm,
    out_ref,
    mid_ref,
    all_info,
    rows_ref,
    gate_buf,
    up_buf,
    down_buf,
    hidden,
    k_all,
    v_all,
    ow,
    att,
    part_send,
    part_recv,
    far_send,
    far_recv,
    stat_recv,
    tok,
    ow_sem,
    gate_sem,
    up_sem,
    down_sem,
    kv_send,
    kv_recv,
    part_ss,
    part_rs,
    far_sem,
    stat_ss,
    stat_rs,
    tok_ss,
    tok_rs,
):
    tokens, width = q_ref.shape
    half_rows = tokens // 2
    c, t, sib, far, diag, others = peers(n)
    weight_copy = pltpu.make_async_copy(ow_hbm, ow, ow_sem)
    weight_copy.start()
    tile = gate_buf.shape[2]
    steps = gate_hbm.shape[2] // tile
    out_steps = D // OUT_TILE
    ring, out_ring = gate_buf.shape[0], down_buf.shape[0]

    def wide_copies(i, slot):
        cols = pl.ds(pl.multiple_of(i * tile, 128), tile)
        return (
            pltpu.make_async_copy(gate_hbm.at[0, :, cols], gate_buf.at[slot], gate_sem.at[slot]),
            pltpu.make_async_copy(up_hbm.at[0, :, cols], up_buf.at[slot], up_sem.at[slot]),
        )

    def down_copy(i, slot):
        cols = pl.ds(pl.multiple_of(i * OUT_TILE, 128), OUT_TILE)
        return pltpu.make_async_copy(
            down_hbm.at[0, :, cols], down_buf.at[slot], down_sem.at[slot]
        )

    for i in range(ring):
        for copy in wide_copies(i, i):
            copy.start()
    for i in range(out_ring):
        down_copy(i, i).start()
    enter(n, (sib, far, diag), others)

    k_all[c] = k_ref[...]
    v_all[c] = v_ref[...]
    before = (
        lax.broadcasted_iota(jnp.int32, (tokens, tokens), 0)
        < lax.broadcasted_iota(jnp.int32, (tokens, tokens), 1)
    ).astype(f32).astype(bf16)
    info = info_ref[...]
    slots = jnp.dot(info.astype(bf16), before, preferred_element_type=f32)
    slots = jnp.where(info > 0.5, slots, -1.0)
    row = lax.broadcasted_iota(jnp.int32, info.shape, 0)
    all_info[c] = jnp.where(row == 0, slots, info)
    kv_copies = []
    for i, o in enumerate(others):
        for j, ref in enumerate((k_all, v_all, all_info)):
            copy = remote(ref.at[c], ref.at[c], kv_send.at[i, j], kv_recv.at[c, j], ctx=o)
            copy.start()
            kv_copies.append(copy)
    for o in others:
        for j, ref in enumerate((k_all, v_all, all_info)):
            remote(ref.at[o], ref.at[o], kv_send.at[0, j], kv_recv.at[o, j], ctx=o).wait_recv()

    keys = k_all[...].reshape(n * tokens, HD)
    values = v_all[...].reshape(n * tokens, HD)
    allowed = lax.broadcasted_iota(
        jnp.int32, (tokens, n * tokens), 1
    ) <= c * tokens + lax.broadcasted_iota(jnp.int32, (tokens, n * tokens), 0)
    for h in range(width // HD):
        scores = lax.dot_general(
            q_ref[:, h * HD : (h + 1) * HD],
            keys,
            (((1,), (1,)), ((), ())),
            preferred_element_type=f32,
        ) * (1.0 / math.sqrt(HD))
        scores = jnp.where(allowed, scores, masked_score)
        weights = jnp.exp(scores - jnp.max(scores, axis=1, keepdims=True))
        total = jnp.sum(weights, axis=1, keepdims=True)
        weighted = jnp.dot(weights.astype(bf16), values, preferred_element_type=f32)
        att[:, h * HD : (h + 1) * HD] = (weighted / total).astype(bf16)

    weight_copy.wait()

    def partial(block):
        cols = pl.ds(pl.multiple_of(block * width, 128), width)
        return jnp.dot(att[...], ow[:, cols], preferred_element_type=f32)

    sib_copies = []
    for j, block in enumerate((diag, sib)):
        part_send[j] = partial(block).astype(bf16)
        copy = remote(
            part_send.at[j], part_recv.at[j], part_ss.at[j], part_rs.at[j], tp=sib
        )
        copy.start()
        sib_copies.append(copy)
    keep = partial(far)
    sib_copies[0].wait()
    far_send[...] = (keep + part_recv[0].astype(f32)).astype(bf16)
    far_copy = remote(far_send, far_recv, far_sem.at[0], far_sem.at[1], tp=far)
    far_copy.start()
    own = partial(t)
    sib_copies[1].wait()
    own = own + part_recv[1].astype(f32)
    far_copy.wait()
    own = own + far_recv[...].astype(f32)

    residual = res_ref[...].astype(f32)
    gained = ag_ref[...][None, :] * own
    stat_recv[t] = columns_to_rows(
        [
            jnp.sum(own * own, axis=1, keepdims=True),
            jnp.sum(residual * residual, axis=1, keepdims=True),
            jnp.sum(residual * gained, axis=1, keepdims=True),
            jnp.sum(gained * gained, axis=1, keepdims=True),
        ],
        tokens,
    )
    stat_copies = []
    for i, p in enumerate((far, diag, sib)):
        copy = remote(stat_recv.at[t], stat_recv.at[t], stat_ss.at[i], stat_rs.at[t], tp=p)
        copy.start()
        stat_copies.append(copy)
    for i, p in enumerate((far, diag, sib)):
        remote(stat_recv.at[p], stat_recv.at[p], stat_ss.at[i], stat_rs.at[p], tp=p).wait_recv()
    sums = rows_to_columns(stat_recv[0] + stat_recv[1] + stat_recv[2] + stat_recv[3])
    scale = lax.rsqrt(sums[:, 0:1] / D + epsilon)
    squares = sums[:, 1:2] + 2.0 * scale * sums[:, 2:3] + scale * scale * sums[:, 3:4]
    middle = residual + gained * scale
    mid_ref[...] = middle
    tok[c, t] = (
        mg_ref[...][None, :] * middle * lax.rsqrt(jnp.maximum(squares, 0.0) / D + epsilon)
    ).astype(bf16)

    sent = []

    def piece(cb, tb, half):
        return tok.at[cb, tb, pl.ds(half * half_rows, half_rows)]

    def push(cb, tb, half, **where):
        ref = piece(cb, tb, half)
        copy = remote(ref, ref, tok_ss.at[len(sent)], tok_rs.at[cb, tb, half], **where)
        copy.start()
        sent.append(copy)

    def arrive(cb, tb, half):
        ref = piece(cb, tb, half)
        remote(ref, ref, tok_ss.at[0], tok_rs.at[cb, tb, half], tp=sib).wait_recv()

    for half in (0, 1):
        for o in others:
            push(c, t, half, ctx=o)
        push(c, t, 1 - half, tp=far)
    for half in (0, 1):
        push(c, t, half, tp=sib)
    for o in others:
        arrive(o, t, 0)
        push(o, t, 0, tp=far)
        push(o, t, 0, tp=sib)
    arrive(c, far, 1)
    for o in others:
        push(c, far, 1, ctx=o)
    push(c, far, 1, tp=sib)
    for o in others:
        arrive(o, t, 1)
        push(o, t, 1, tp=sib)
    arrive(c, far, 0)
    push(c, far, 0, tp=sib)
    for o in others:
        for half in (0, 1):
            arrive(o, far, half)
            push(o, far, half, tp=sib)
    for b in [c] + others:
        for block in (sib, diag):
            for half in (0, 1):
                arrive(b, block, half)
    gates = []
    for b in range(n):
        chosen = (
            lax.broadcasted_iota(jnp.int32, (CAP, tokens), 0).astype(f32) == all_info[b, 0:1, :]
        )
        gates.append(
            jnp.sum(jnp.where(chosen, all_info[b, 1:2, :], 0.0), axis=1, keepdims=True)
        )
        table = chosen.astype(f32).astype(bf16)
        for block in range(TP):
            rows_ref[b * CAP : (b + 1) * CAP, block * width : (block + 1) * width] = jnp.dot(
                table, tok[b, block], preferred_element_type=f32
            ).astype(bf16)
    row_gate = jnp.concatenate(gates, axis=0)

    @pl.loop(0, steps)
    def _(i):
        slot = i % ring
        for copy in wide_copies(i, slot):
            copy.wait()
        gate_part = jnp.dot(rows_ref[...], gate_buf[slot], preferred_element_type=f32)
        up_part = jnp.dot(rows_ref[...], up_buf[slot], preferred_element_type=f32)
        hidden[:, pl.ds(pl.multiple_of(i * tile, 128), tile)] = (
            gate_part / (1.0 + jnp.exp(-gate_part)) * up_part
        ).astype(bf16)

        @pl.when(i + ring < steps)
        def _():
            for copy in wide_copies(i + ring, slot):
                copy.start()

    @pl.loop(0, out_steps)
    def _(i):
        slot = i % out_ring
        down_copy(i, slot).wait()
        out_ref[:, pl.ds(pl.multiple_of(i * OUT_TILE, 128), OUT_TILE)] = (
            jnp.dot(hidden[...], down_buf[slot], preferred_element_type=f32) * row_gate
        ).astype(bf16)

        @pl.when(i + out_ring < out_steps)
        def _():
            down_copy(i + out_ring, slot).start()

    for copy in kv_copies + stat_copies + sent:
        copy.wait_send()


def front(n, queries, key_rows, value_rows, residual, out_weight, ag, mg, info, gate, up, down):
    tokens, width = queries.shape
    units = gate.shape[2]
    tile, ring, out_ring = (512, 4, 3) if units >= 4096 else (256, 1, 2)
    vmem = pl.BlockSpec(memory_space=pltpu.VMEM)
    hbm = pl.BlockSpec(memory_space=pl.ANY)
    dma = pltpu.SemaphoreType.DMA
    pushes = 2 * (n - 1) + 2 + 2 + 2 * (n - 1) + (n - 1) + 1 + (n - 1) + 1 + 2 * (n - 1)
    return pl.pallas_call(
        functools.partial(front_kernel, n),
        out_shape=(
            jax.ShapeDtypeStruct((n * CAP, D), bf16),
            jax.ShapeDtypeStruct((tokens, width), f32),
            jax.ShapeDtypeStruct((n, 8, tokens), f32),
        ),
        in_specs=[vmem] * 4 + [hbm] + [vmem] * 3 + [hbm] * 3,
        out_specs=(vmem, vmem, vmem),
        scratch_shapes=[
            pltpu.VMEM((n * CAP, D), bf16),
            pltpu.VMEM((ring, D, tile), bf16),
            pltpu.VMEM((ring, D, tile), bf16),
            pltpu.VMEM((out_ring, units, OUT_TILE), bf16),
            pltpu.VMEM((n * CAP, units), bf16),
            pltpu.VMEM((n, tokens, HD), bf16),
            pltpu.VMEM((n, tokens, HD), bf16),
            pltpu.VMEM(out_weight.shape, bf16),
            pltpu.VMEM((tokens, width), bf16),
            pltpu.VMEM((2, tokens, width), bf16),
            pltpu.VMEM((2, tokens, width), bf16),
            pltpu.VMEM((tokens, width), bf16),
            pltpu.VMEM((tokens, width), bf16),
            pltpu.VMEM((TP, 8, tokens), f32),
            pltpu.VMEM((n, TP, tokens, width), bf16),
            dma,
            dma((ring,)),
            dma((ring,)),
            dma((out_ring,)),
            dma((max(n - 1, 1), 3)),
            dma((n, 3)),
            dma((2,)),
            dma((2,)),
            dma((2,)),
            dma((3,)),
            dma((TP,)),
            dma((pushes,)),
            dma((n, TP, 2)),
        ],
        compiler_params=pltpu.CompilerParams(
            collective_id=0, has_side_effects=True, vmem_limit_bytes=VMEM_LIMIT
        ),
        name="front",
    )(queries, key_rows, value_rows, residual, out_weight, ag, mg, info, gate, up, down)


def back_kernel(
    n,
    por_ref,
    info_ref,
    mid_ref,
    og_ref,
    out_ref,
    one_send,
    one_recv,
    sums,
    two_send,
    turn_far,
    turn_ctx,
    from_far,
    from_ctx,
    stat_recv,
    one_ss,
    one_rs,
    two_ss,
    turn_far_rs,
    turn_ctx_rs,
    from_far_rs,
    from_ctx_rs,
    stat_ss,
    stat_rs,
):
    tokens, width = mid_ref.shape
    half_rows = tokens // 2
    first, second = pl.ds(0, half_rows), pl.ds(half_rows, half_rows)
    c, t, sib, far, diag, others = peers(n)
    enter(n, (sib, far, diag), others)

    def spread(b):
        slot = rows_to_columns(info_ref[b])[:, 0:1]
        return (
            lax.broadcasted_iota(jnp.int32, (tokens, CAP), 1).astype(f32) == slot
        ).astype(f32).astype(bf16)

    def partial(table, b, block):
        cols = pl.ds(pl.multiple_of(block * width, 128), width)
        return jnp.dot(table, por_ref[b, :, cols], preferred_element_type=f32)

    copies = []

    def push(src, dst, ss, rs, **where):
        copy = remote(src, dst, ss, rs, **where)
        copy.start()
        copies.append(copy)

    order = others + [c]
    tables = [spread(b) for b in order]
    for j, block in ((1, diag), (0, sib)):
        for i, b in enumerate(order):
            one_send[b, j] = partial(tables[i], b, block).astype(bf16)
            push(one_send.at[b, j], one_recv.at[b, j], one_ss.at[i, j], one_rs.at[b, j], tp=sib)
    for j, block in ((1, far), (0, t)):
        for i, b in enumerate(order):
            own = partial(tables[i], b, block)
            remote(
                one_send.at[b, j], one_recv.at[b, j], one_ss.at[i, j], one_rs.at[b, j], tp=sib
            ).wait_recv()
            own = own + one_recv[b, j].astype(f32)
            sums[b, j] = own
            if i < n - 1:
                two_send[b, j] = own.astype(bf16)
                if j == 1:
                    push(
                        two_send.at[b, 1, first],
                        turn_far.at[b],
                        two_ss.at[i, 0],
                        turn_far_rs.at[b],
                        tp=far,
                    )
                    push(
                        two_send.at[b, 1, second],
                        turn_ctx.at[c],
                        two_ss.at[i, 1],
                        turn_ctx_rs.at[c],
                        ctx=b,
                    )
                else:
                    push(
                        two_send.at[b, 0, second],
                        from_ctx.at[c, second],
                        two_ss.at[i, 2],
                        from_ctx_rs.at[c, 1],
                        ctx=b,
                    )
            elif j == 1:
                two_send[c, 1, first] = own[:half_rows].astype(bf16)
                push(
                    two_send.at[c, 1, first],
                    from_far.at[first],
                    two_ss.at[i, 0],
                    from_far_rs.at[0],
                    tp=far,
                )
    for i, b in enumerate(others):
        remote(
            two_send.at[b, 1, first], turn_far.at[b], two_ss.at[i, 0], turn_far_rs.at[b], tp=far
        ).wait_recv()
        two_send[b, 0, first] = (sums[b, 0, first] + turn_far[b].astype(f32)).astype(bf16)
        push(
            two_send.at[b, 0, first],
            from_ctx.at[c, first],
            two_ss.at[i, 3],
            from_ctx_rs.at[c, 0],
            ctx=b,
        )
    turned = sums[c, 1, second]
    for i, b in enumerate(others):
        remote(
            two_send.at[b, 1, second], turn_ctx.at[b], two_ss.at[i, 1], turn_ctx_rs.at[b], ctx=b
        ).wait_recv()
        turned = turned + turn_ctx[b].astype(f32)
    two_send[c, 1, second] = turned.astype(bf16)
    push(
        two_send.at[c, 1, second],
        from_far.at[second],
        two_ss.at[n - 1, 1],
        from_far_rs.at[1],
        tp=far,
    )
    mixture = sums[c, 0]
    for b in others:
        for half, rows in ((1, second), (0, first)):
            remote(
                two_send.at[b, 0, rows],
                from_ctx.at[b, rows],
                two_ss.at[0, 2],
                from_ctx_rs.at[b, half],
                ctx=b,
            ).wait_recv()
        mixture = mixture + from_ctx[b].astype(f32)
    for half, rows in ((0, first), (1, second)):
        remote(
            two_send.at[c, 1, rows],
            from_far.at[rows],
            two_ss.at[0, 0],
            from_far_rs.at[half],
            tp=far,
        ).wait_recv()
    mixture = mixture + from_far[...].astype(f32)

    stat_recv[t] = columns_to_rows(
        [jnp.sum(mixture * mixture, axis=1, keepdims=True)], tokens
    )
    for i, p in enumerate((far, diag, sib)):
        push(stat_recv.at[t], stat_recv.at[t], stat_ss.at[i], stat_rs.at[t], tp=p)
    for i, p in enumerate((far, diag, sib)):
        remote(stat_recv.at[p], stat_recv.at[p], stat_ss.at[i], stat_rs.at[p], tp=p).wait_recv()
    squares = rows_to_columns(stat_recv[0] + stat_recv[1] + stat_recv[2] + stat_recv[3])[:, 0:1]
    normed = og_ref[...][None, :] * mixture * lax.rsqrt(squares / D + epsilon)
    out_ref[...] = (mid_ref[...] + normed).astype(bf16)
    for copy in copies:
        copy.wait_send()


def back(n, portions, info, middle, og):
    tokens, width = middle.shape
    vmem = pl.BlockSpec(memory_space=pltpu.VMEM)
    dma = pltpu.SemaphoreType.DMA
    return pl.pallas_call(
        functools.partial(back_kernel, n),
        out_shape=jax.ShapeDtypeStruct((tokens, width), bf16),
        in_specs=[vmem] * 4,
        out_specs=vmem,
        scratch_shapes=[
            pltpu.VMEM((n, 2, tokens, width), bf16),
            pltpu.VMEM((n, 2, tokens, width), bf16),
            pltpu.VMEM((n, 2, tokens, width), f32),
            pltpu.VMEM((n, 2, tokens, width), bf16),
            pltpu.VMEM((n, tokens // 2, width), bf16),
            pltpu.VMEM((n, tokens // 2, width), bf16),
            pltpu.VMEM((tokens, width), bf16),
            pltpu.VMEM((n, tokens, width), bf16),
            pltpu.VMEM((TP, 8, tokens), f32),
            dma((n, 2)),
            dma((n, 2)),
            dma((n, 4)),
            dma((n,)),
            dma((n,)),
            dma((2,)),
            dma((n, 2)),
            dma((3,)),
            dma((TP,)),
        ],
        compiler_params=pltpu.CompilerParams(
            collective_id=1, has_side_effects=True, vmem_limit_bytes=VMEM_LIMIT
        ),
        name="back",
    )(portions, info, middle, og)


def shards(
    n,
    queries,
    key_rows,
    value_rows,
    residual,
    out_weight,
    attention_gain,
    middle_gain,
    output_gain,
    gate_weight,
    up_weight,
    down_weight,
    routes,
    gate_shares,
):
    tokens = queries.shape[0]
    mine = routes == lax.axis_index("tp")
    named = jnp.sum(mine.astype(f32), axis=1)
    gate = jnp.sum(jnp.where(mine, gate_shares, 0.0), axis=1)
    row = jnp.arange(8, dtype=jnp.int32)[:, None]
    info = jnp.where(row == 0, named[None, :], jnp.where(row == 1, gate[None, :], 0.0))
    portions, middle, info = front(
        n,
        queries,
        key_rows,
        value_rows,
        residual,
        out_weight,
        attention_gain,
        middle_gain,
        info,
        gate_weight,
        up_weight,
        down_weight,
    )
    return back(n, portions.reshape(n, CAP, D), info, middle, output_gain)


def solution(mesh):
    in_specs = (
        P(("dp", "ctx"), "tp"),
        P(("dp", "ctx"), "tp"),
        P(("dp", "ctx"), "tp"),
        P(("dp", "ctx"), "tp"),
        P("tp", None),
        P("tp"),
        P("tp"),
        P("tp"),
        P("tp", None, "ctx"),
        P("tp", None, "ctx"),
        P("tp", "ctx", None),
        P(("dp", "ctx"), None),
        P(("dp", "ctx"), None),
    )
    out_specs = P(("dp", "ctx"), "tp")
    return jax.shard_map(
        functools.partial(shards, mesh.shape["ctx"]),
        mesh=mesh,
        in_specs=in_specs,
        out_specs=out_specs,
        check_vma=False,
    )
```

```python
import functools
import math

import jax
import jax.numpy as jnp
from jax import lax
from jax.experimental import pallas as pl
from jax.experimental.pallas import tpu as pltpu
from jax.sharding import PartitionSpec as P

D = 3072
HD = 128
TP = 4
CAP = 160

epsilon = 1e-06
masked_score = -1e30
VMEM_LIMIT = 62 << 20
OUT_TILE = 384
f32 = jnp.float32
bf16 = jnp.bfloat16


def peers(n):
    c = lax.axis_index("ctx")
    t = lax.axis_index("tp")
    sib = t + 1 - 2 * (t % 2)
    far = (t + 2) % TP
    diag = TP - 1 - t
    others = [(c + d) % n for d in range(1, n)]
    return c, t, sib, far, diag, others


def remote(src, dst, send_sem, recv_sem, **where):
    return pltpu.make_async_remote_copy(
        src_ref=src,
        dst_ref=dst,
        send_sem=send_sem,
        recv_sem=recv_sem,
        device_id=where,
        device_id_type=pl.DeviceIdType.MESH,
    )


def enter(n, tp_peers, others):
    barrier = pltpu.get_barrier_semaphore()
    for p in tp_peers:
        pl.semaphore_signal(barrier, inc=1, device_id={"tp": p}, device_id_type=pl.DeviceIdType.MESH)
    for o in others:
        pl.semaphore_signal(barrier, inc=1, device_id={"ctx": o}, device_id_type=pl.DeviceIdType.MESH)
    pl.semaphore_wait(barrier, len(tp_peers) + len(others))


def columns_to_rows(columns, tokens):
    lane = lax.broadcasted_iota(jnp.int32, (tokens, 128), 1)
    packed = jnp.zeros((tokens, 128), f32)
    for i, column in enumerate(columns):
        packed = jnp.where(lane == i, column, packed)
    return packed.T[:8]


def rows_to_columns(rows):
    return jnp.concatenate([rows, jnp.zeros((120, rows.shape[1]), f32)], axis=0).T


def front_kernel(
    n,
    q_ref,
    k_ref,
    v_ref,
    res_ref,
    ow_hbm,
    ag_ref,
    mg_ref,
    info_ref,
    gate_hbm,
    up_hbm,
    down_hbm,
    out_ref,
    mid_ref,
    all_info,
    rows_ref,
    gate_buf,
    up_buf,
    down_buf,
    hidden,
    k_all,
    v_all,
    ow,
    att,
    part_send,
    part_recv,
    far_send,
    far_recv,
    stat_recv,
    tok,
    ow_sem,
    gate_sem,
    up_sem,
    down_sem,
    kv_send,
    kv_recv,
    part_ss,
    part_rs,
    far_sem,
    stat_ss,
    stat_rs,
    tok_ss,
    tok_rs,
    tail=None,
):
    tokens, width = q_ref.shape
    half_rows = tokens // 2
    c, t, sib, far, diag, others = peers(n)
    weight_copy = pltpu.make_async_copy(ow_hbm, ow, ow_sem)
    weight_copy.start()
    tile = gate_buf.shape[2]
    steps = gate_hbm.shape[2] // tile
    ring = gate_buf.shape[0]
    halves = width // OUT_TILE
    block_order = (diag, sib, far, t)

    def wide_copies(i, slot):
        cols = pl.ds(pl.multiple_of(i * tile, 128), tile)
        return (
            pltpu.make_async_copy(gate_hbm.at[0, :, cols], gate_buf.at[slot], gate_sem.at[slot]),
            pltpu.make_async_copy(up_hbm.at[0, :, cols], up_buf.at[slot], up_sem.at[slot]),
        )

    def down_cols(block, h):
        return pl.ds(pl.multiple_of(block * width + h * OUT_TILE, 128), OUT_TILE)

    def down_copy(block, h):
        return pltpu.make_async_copy(
            down_hbm.at[0, :, down_cols(block, h)], down_buf.at[h], down_sem.at[h]
        )

    for i in range(ring):
        for copy in wide_copies(i, i):
            copy.start()
    for h in range(halves):
        down_copy(block_order[0], h).start()
    enter(n, (sib, far, diag), others)

    k_all[c] = k_ref[...]
    v_all[c] = v_ref[...]
    before = (
        lax.broadcasted_iota(jnp.int32, (tokens, tokens), 0)
        < lax.broadcasted_iota(jnp.int32, (tokens, tokens), 1)
    ).astype(f32).astype(bf16)
    info = info_ref[...]
    slots = jnp.dot(info.astype(bf16), before, preferred_element_type=f32)
    slots = jnp.where(info > 0.5, slots, -1.0)
    row = lax.broadcasted_iota(jnp.int32, info.shape, 0)
    all_info[c] = jnp.where(row == 0, slots, info)
    kv_copies = []
    for i, o in enumerate(others):
        for j, ref in enumerate((k_all, v_all, all_info)):
            copy = remote(ref.at[c], ref.at[c], kv_send.at[i, j], kv_recv.at[c, j], ctx=o)
            copy.start()
            kv_copies.append(copy)
    for o in others:
        for j, ref in enumerate((k_all, v_all, all_info)):
            remote(ref.at[o], ref.at[o], kv_send.at[0, j], kv_recv.at[o, j], ctx=o).wait_recv()

    keys = k_all[...].reshape(n * tokens, HD)
    values = v_all[...].reshape(n * tokens, HD)
    allowed = lax.broadcasted_iota(
        jnp.int32, (tokens, n * tokens), 1
    ) <= c * tokens + lax.broadcasted_iota(jnp.int32, (tokens, n * tokens), 0)
    for h in range(width // HD):
        scores = lax.dot_general(
            q_ref[:, h * HD : (h + 1) * HD],
            keys,
            (((1,), (1,)), ((), ())),
            preferred_element_type=f32,
        ) * (1.0 / math.sqrt(HD))
        scores = jnp.where(allowed, scores, masked_score)
        weights = jnp.exp(scores - jnp.max(scores, axis=1, keepdims=True))
        total = jnp.sum(weights, axis=1, keepdims=True)
        weighted = jnp.dot(weights.astype(bf16), values, preferred_element_type=f32)
        att[:, h * HD : (h + 1) * HD] = (weighted / total).astype(bf16)

    weight_copy.wait()

    def partial(block):
        cols = pl.ds(pl.multiple_of(block * width, 128), width)
        return jnp.dot(att[...], ow[:, cols], preferred_element_type=f32)

    sib_copies = []
    for j, block in enumerate((diag, sib)):
        part_send[j] = partial(block).astype(bf16)
        copy = remote(
            part_send.at[j], part_recv.at[j], part_ss.at[j], part_rs.at[j], tp=sib
        )
        copy.start()
        sib_copies.append(copy)
    keep = partial(far)
    sib_copies[0].wait()
    far_send[...] = (keep + part_recv[0].astype(f32)).astype(bf16)
    far_copy = remote(far_send, far_recv, far_sem.at[0], far_sem.at[1], tp=far)
    far_copy.start()
    own = partial(t)
    sib_copies[1].wait()
    own = own + part_recv[1].astype(f32)
    far_copy.wait()
    own = own + far_recv[...].astype(f32)

    residual = res_ref[...].astype(f32)
    gained = ag_ref[...][None, :] * own
    stat_recv[t] = columns_to_rows(
        [
            jnp.sum(own * own, axis=1, keepdims=True),
            jnp.sum(residual * residual, axis=1, keepdims=True),
            jnp.sum(residual * gained, axis=1, keepdims=True),
            jnp.sum(gained * gained, axis=1, keepdims=True),
        ],
        tokens,
    )
    stat_copies = []
    for i, p in enumerate((far, diag, sib)):
        copy = remote(stat_recv.at[t], stat_recv.at[t], stat_ss.at[i], stat_rs.at[t], tp=p)
        copy.start()
        stat_copies.append(copy)
    for i, p in enumerate((far, diag, sib)):
        remote(stat_recv.at[p], stat_recv.at[p], stat_ss.at[i], stat_rs.at[p], tp=p).wait_recv()
    sums = rows_to_columns(stat_recv[0] + stat_recv[1] + stat_recv[2] + stat_recv[3])
    scale = lax.rsqrt(sums[:, 0:1] / D + epsilon)
    squares = sums[:, 1:2] + 2.0 * scale * sums[:, 2:3] + scale * scale * sums[:, 3:4]
    middle = residual + gained * scale
    mid_ref[...] = middle
    tok[c, t] = (
        mg_ref[...][None, :] * middle * lax.rsqrt(jnp.maximum(squares, 0.0) / D + epsilon)
    ).astype(bf16)

    sent = []

    def piece(cb, tb, half):
        return tok.at[cb, tb, pl.ds(half * half_rows, half_rows)]

    def push(cb, tb, half, **where):
        ref = piece(cb, tb, half)
        copy = remote(ref, ref, tok_ss.at[len(sent)], tok_rs.at[cb, tb, half], **where)
        copy.start()
        sent.append(copy)

    def arrive(cb, tb, half):
        ref = piece(cb, tb, half)
        remote(ref, ref, tok_ss.at[0], tok_rs.at[cb, tb, half], tp=sib).wait_recv()

    for half in (0, 1):
        for o in others:
            push(c, t, half, ctx=o)
        push(c, t, 1 - half, tp=far)
    for half in (0, 1):
        push(c, t, half, tp=sib)
    for o in others:
        arrive(o, t, 0)
        push(o, t, 0, tp=far)
        push(o, t, 0, tp=sib)
    arrive(c, far, 1)
    for o in others:
        push(c, far, 1, ctx=o)
    push(c, far, 1, tp=sib)
    for o in others:
        arrive(o, t, 1)
        push(o, t, 1, tp=sib)
    arrive(c, far, 0)
    push(c, far, 0, tp=sib)
    for o in others:
        for half in (0, 1):
            arrive(o, far, half)
            push(o, far, half, tp=sib)
    for b in [c] + others:
        for block in (sib, diag):
            for half in (0, 1):
                arrive(b, block, half)
    gates = []
    for b in range(n):
        chosen = (
            lax.broadcasted_iota(jnp.int32, (CAP, tokens), 0).astype(f32) == all_info[b, 0:1, :]
        )
        gates.append(
            jnp.sum(jnp.where(chosen, all_info[b, 1:2, :], 0.0), axis=1, keepdims=True)
        )
        table = chosen.astype(f32).astype(bf16)
        for block in range(TP):
            rows_ref[b * CAP : (b + 1) * CAP, block * width : (block + 1) * width] = jnp.dot(
                table, tok[b, block], preferred_element_type=f32
            ).astype(bf16)
    row_gate = jnp.concatenate(gates, axis=0)

    @pl.loop(0, steps)
    def _(i):
        slot = i % ring
        for copy in wide_copies(i, slot):
            copy.wait()
        gate_part = jnp.dot(rows_ref[...], gate_buf[slot], preferred_element_type=f32)
        up_part = jnp.dot(rows_ref[...], up_buf[slot], preferred_element_type=f32)
        hidden[:, pl.ds(pl.multiple_of(i * tile, 128), tile)] = (
            gate_part / (1.0 + jnp.exp(-gate_part)) * up_part
        ).astype(bf16)

        @pl.when(i + ring < steps)
        def _():
            for copy in wide_copies(i + ring, slot):
                copy.start()

    stages = tail() if tail else iter(())
    next(stages, None)
    for at, block in enumerate(block_order):

        @pl.loop(0, halves)
        def _(h):
            down_copy(block, h).wait()
            portion = (
                jnp.dot(hidden[...], down_buf[h], preferred_element_type=f32) * row_gate
            ).astype(bf16)
            for b in range(n):
                out_ref[b, :, down_cols(block, h)] = portion[b * CAP : (b + 1) * CAP]
            if at + 1 < TP:
                down_copy(block_order[at + 1], h).start()

        next(stages, None)

    for copy in kv_copies + stat_copies + sent:
        copy.wait_send()


def front(n, fused, queries, key_rows, value_rows, residual, out_weight, ag, mg, info, gate, up, down, og):
    tokens, width = queries.shape
    units = gate.shape[2]
    tile, ring = (512, 3 if fused else 4) if units >= 4096 else (256, 1)
    halves = width // OUT_TILE
    vmem = pl.BlockSpec(memory_space=pltpu.VMEM)
    hbm = pl.BlockSpec(memory_space=pl.ANY)
    dma = pltpu.SemaphoreType.DMA
    pushes = 2 * (n - 1) + 2 + 2 + 2 * (n - 1) + (n - 1) + 1 + (n - 1) + 1 + 2 * (n - 1)
    inputs = [vmem] * 4 + [hbm] + [vmem] * 3 + [hbm] * 3
    made = (((n, CAP, D), bf16), ((tokens, width), f32), ((n, 8, tokens), f32))
    if fused:
        kernel = functools.partial(fused_kernel, n)
        outputs = jax.ShapeDtypeStruct((tokens, width), bf16)
        inputs.append(vmem)
        before = [pltpu.VMEM(*m) for m in made]
        after = back_scratch(n, tokens, width)
    else:
        kernel = functools.partial(front_kernel, n)
        outputs = tuple(jax.ShapeDtypeStruct(*m) for m in made)
        before = after = []
    return pl.pallas_call(
        kernel,
        out_shape=outputs,
        in_specs=inputs,
        out_specs=vmem if fused else (vmem,) * 3,
        scratch_shapes=before
        + [
            pltpu.VMEM((n * CAP, D), bf16),
            pltpu.VMEM((ring, D, tile), bf16),
            pltpu.VMEM((ring, D, tile), bf16),
            pltpu.VMEM((halves, units, OUT_TILE), bf16),
            pltpu.VMEM((n * CAP, units), bf16),
            pltpu.VMEM((n, tokens, HD), bf16),
            pltpu.VMEM((n, tokens, HD), bf16),
            pltpu.VMEM(out_weight.shape, bf16),
            pltpu.VMEM((tokens, width), bf16),
            pltpu.VMEM((2, tokens, width), bf16),
            pltpu.VMEM((2, tokens, width), bf16),
            pltpu.VMEM((tokens, width), bf16),
            pltpu.VMEM((tokens, width), bf16),
            pltpu.VMEM((TP, 8, tokens), f32),
            pltpu.VMEM((n, TP, tokens, width), bf16),
            dma,
            dma((ring,)),
            dma((ring,)),
            dma((halves,)),
            dma((max(n - 1, 1), 3)),
            dma((n, 3)),
            dma((2,)),
            dma((2,)),
            dma((2,)),
            dma((3,)),
            dma((TP,)),
            dma((pushes,)),
            dma((n, TP, 2)),
        ]
        + after,
        compiler_params=pltpu.CompilerParams(
            collective_id=0, has_side_effects=True, vmem_limit_bytes=VMEM_LIMIT
        ),
        name="front",
    )(queries, key_rows, value_rows, residual, out_weight, ag, mg, info, gate, up, down, *([og] if fused else []))


BACK_SCRATCH = 18


def back_scratch(n, tokens, width):
    dma = pltpu.SemaphoreType.DMA
    return [
        pltpu.VMEM((n, 2, tokens, width), bf16),
        pltpu.VMEM((n, 2, tokens, width), bf16),
        pltpu.VMEM((n, 2, tokens, width), f32),
        pltpu.VMEM((n, 2, tokens, width), bf16),
        pltpu.VMEM((n, tokens // 2, width), bf16),
        pltpu.VMEM((n, tokens // 2, width), bf16),
        pltpu.VMEM((tokens, width), bf16),
        pltpu.VMEM((n, tokens, width), bf16),
        pltpu.VMEM((TP, 8, tokens), f32),
        dma((n, 2)),
        dma((n, 2)),
        dma((n, 4)),
        dma((n,)),
        dma((n,)),
        dma((2,)),
        dma((n, 2)),
        dma((3,)),
        dma((TP,)),
    ]


def back_stages(
    n,
    por_ref,
    info_ref,
    mid_ref,
    og_ref,
    out_ref,
    one_send,
    one_recv,
    sums,
    two_send,
    turn_far,
    turn_ctx,
    from_far,
    from_ctx,
    stat_recv,
    one_ss,
    one_rs,
    two_ss,
    turn_far_rs,
    turn_ctx_rs,
    from_far_rs,
    from_ctx_rs,
    stat_ss,
    stat_rs,
):
    tokens, width = mid_ref.shape
    half_rows = tokens // 2
    first, second = pl.ds(0, half_rows), pl.ds(half_rows, half_rows)
    c, t, sib, far, diag, others = peers(n)

    def spread(b):
        slot = rows_to_columns(info_ref[b])[:, 0:1]
        return (
            lax.broadcasted_iota(jnp.int32, (tokens, CAP), 1).astype(f32) == slot
        ).astype(f32).astype(bf16)

    def partial(table, b, block):
        cols = pl.ds(pl.multiple_of(block * width, 128), width)
        return jnp.dot(table, por_ref[b, :, cols], preferred_element_type=f32)

    copies = []

    def push(src, dst, ss, rs, **where):
        copy = remote(src, dst, ss, rs, **where)
        copy.start()
        copies.append(copy)

    order = others + [c]
    tables = [spread(b) for b in order]
    for j, block in ((1, diag), (0, sib)):
        yield
        for i, b in enumerate(order):
            one_send[b, j] = partial(tables[i], b, block).astype(bf16)
            push(one_send.at[b, j], one_recv.at[b, j], one_ss.at[i, j], one_rs.at[b, j], tp=sib)
    for j, block in ((1, far), (0, t)):
        yield
        for i, b in enumerate(order):
            own = partial(tables[i], b, block)
            remote(
                one_send.at[b, j], one_recv.at[b, j], one_ss.at[i, j], one_rs.at[b, j], tp=sib
            ).wait_recv()
            own = own + one_recv[b, j].astype(f32)
            sums[b, j] = own
            if i < n - 1:
                two_send[b, j] = own.astype(bf16)
                if j == 1:
                    push(
                        two_send.at[b, 1, first],
                        turn_far.at[b],
                        two_ss.at[i, 0],
                        turn_far_rs.at[b],
                        tp=far,
                    )
                    push(
                        two_send.at[b, 1, second],
                        turn_ctx.at[c],
                        two_ss.at[i, 1],
                        turn_ctx_rs.at[c],
                        ctx=b,
                    )
                else:
                    push(
                        two_send.at[b, 0, second],
                        from_ctx.at[c, second],
                        two_ss.at[i, 2],
                        from_ctx_rs.at[c, 1],
                        ctx=b,
                    )
            elif j == 1:
                two_send[c, 1, first] = own[:half_rows].astype(bf16)
                push(
                    two_send.at[c, 1, first],
                    from_far.at[first],
                    two_ss.at[i, 0],
                    from_far_rs.at[0],
                    tp=far,
                )
    for i, b in enumerate(others):
        remote(
            two_send.at[b, 1, first], turn_far.at[b], two_ss.at[i, 0], turn_far_rs.at[b], tp=far
        ).wait_recv()
        two_send[b, 0, first] = (sums[b, 0, first] + turn_far[b].astype(f32)).astype(bf16)
        push(
            two_send.at[b, 0, first],
            from_ctx.at[c, first],
            two_ss.at[i, 3],
            from_ctx_rs.at[c, 0],
            ctx=b,
        )
    turned = sums[c, 1, second]
    for i, b in enumerate(others):
        remote(
            two_send.at[b, 1, second], turn_ctx.at[b], two_ss.at[i, 1], turn_ctx_rs.at[b], ctx=b
        ).wait_recv()
        turned = turned + turn_ctx[b].astype(f32)
    two_send[c, 1, second] = turned.astype(bf16)
    push(
        two_send.at[c, 1, second],
        from_far.at[second],
        two_ss.at[n - 1, 1],
        from_far_rs.at[1],
        tp=far,
    )
    mixture = sums[c, 0]
    for b in others:
        for half, rows in ((1, second), (0, first)):
            remote(
                two_send.at[b, 0, rows],
                from_ctx.at[b, rows],
                two_ss.at[0, 2],
                from_ctx_rs.at[b, half],
                ctx=b,
            ).wait_recv()
        mixture = mixture + from_ctx[b].astype(f32)
    for half, rows in ((0, first), (1, second)):
        remote(
            two_send.at[c, 1, rows],
            from_far.at[rows],
            two_ss.at[0, 0],
            from_far_rs.at[half],
            tp=far,
        ).wait_recv()
    mixture = mixture + from_far[...].astype(f32)

    stat_recv[t] = columns_to_rows(
        [jnp.sum(mixture * mixture, axis=1, keepdims=True)], tokens
    )
    for i, p in enumerate((far, diag, sib)):
        push(stat_recv.at[t], stat_recv.at[t], stat_ss.at[i], stat_rs.at[t], tp=p)
    for i, p in enumerate((far, diag, sib)):
        remote(stat_recv.at[p], stat_recv.at[p], stat_ss.at[i], stat_rs.at[p], tp=p).wait_recv()
    squares = rows_to_columns(stat_recv[0] + stat_recv[1] + stat_recv[2] + stat_recv[3])[:, 0:1]
    normed = og_ref[...][None, :] * mixture * lax.rsqrt(squares / D + epsilon)
    out_ref[...] = (mid_ref[...] + normed).astype(bf16)
    for copy in copies:
        copy.wait_send()


def back_kernel(n, *refs):
    c, t, sib, far, diag, others = peers(n)
    enter(n, (sib, far, diag), others)
    for _ in back_stages(n, *refs):
        pass


def fused_kernel(n, *refs):
    inputs, og_ref, out_ref = refs[:11], refs[11], refs[12]
    por_ref, mid_ref, all_info = refs[13:16]
    scratch = refs[16:-BACK_SCRATCH]

    def tail():
        return back_stages(
            n, por_ref, all_info, mid_ref, og_ref, out_ref, *refs[-BACK_SCRATCH:]
        )

    front_kernel(n, *inputs, por_ref, mid_ref, all_info, *scratch, tail=tail)


def back(n, portions, info, middle, og):
    tokens, width = middle.shape
    vmem = pl.BlockSpec(memory_space=pltpu.VMEM)
    return pl.pallas_call(
        functools.partial(back_kernel, n),
        out_shape=jax.ShapeDtypeStruct((tokens, width), bf16),
        in_specs=[vmem] * 4,
        out_specs=vmem,
        scratch_shapes=back_scratch(n, tokens, width),
        compiler_params=pltpu.CompilerParams(
            collective_id=1, has_side_effects=True, vmem_limit_bytes=VMEM_LIMIT
        ),
        name="back",
    )(portions, info, middle, og)


def shards(
    n,
    queries,
    key_rows,
    value_rows,
    residual,
    out_weight,
    attention_gain,
    middle_gain,
    output_gain,
    gate_weight,
    up_weight,
    down_weight,
    routes,
    gate_shares,
):
    tokens = queries.shape[0]
    mine = routes == lax.axis_index("tp")
    named = jnp.sum(mine.astype(f32), axis=1)
    gate = jnp.sum(jnp.where(mine, gate_shares, 0.0), axis=1)
    row = jnp.arange(8, dtype=jnp.int32)[:, None]
    info = jnp.where(row == 0, named[None, :], jnp.where(row == 1, gate[None, :], 0.0))
    fused = n == 2
    result = front(
        n,
        fused,
        queries,
        key_rows,
        value_rows,
        residual,
        out_weight,
        attention_gain,
        middle_gain,
        info,
        gate_weight,
        up_weight,
        down_weight,
        output_gain,
    )
    if fused:
        return result
    portions, middle, info = result
    return back(n, portions, info, middle, output_gain)


def solution(mesh):
    in_specs = (
        P(("dp", "ctx"), "tp"),
        P(("dp", "ctx"), "tp"),
        P(("dp", "ctx"), "tp"),
        P(("dp", "ctx"), "tp"),
        P("tp", None),
        P("tp"),
        P("tp"),
        P("tp"),
        P("tp", None, "ctx"),
        P("tp", None, "ctx"),
        P("tp", "ctx", None),
        P(("dp", "ctx"), None),
        P(("dp", "ctx"), None),
    )
    out_specs = P(("dp", "ctx"), "tp")
    return jax.shard_map(
        functools.partial(shards, mesh.shape["ctx"]),
        mesh=mesh,
        in_specs=in_specs,
        out_specs=out_specs,
        check_vma=False,
    )
```

```python
import functools
import math

import jax
import jax.numpy as jnp
from jax import lax
from jax.experimental import pallas as pl
from jax.experimental.pallas import tpu as pltpu
from jax.sharding import PartitionSpec as P

D = 3072
HD = 128
TP = 4
CAP = 160

epsilon = 1e-06
masked_score = -1e30
VMEM_LIMIT = 62 << 20
OUT_TILE = 384
f32 = jnp.float32
bf16 = jnp.bfloat16


def peers(n):
    c = lax.axis_index("ctx")
    t = lax.axis_index("tp")
    sib = t + 1 - 2 * (t % 2)
    far = (t + 2) % TP
    diag = TP - 1 - t
    others = [(c + d) % n for d in range(1, n)]
    return c, t, sib, far, diag, others


def remote(src, dst, send_sem, recv_sem, **where):
    return pltpu.make_async_remote_copy(
        src_ref=src,
        dst_ref=dst,
        send_sem=send_sem,
        recv_sem=recv_sem,
        device_id=where,
        device_id_type=pl.DeviceIdType.MESH,
    )


def enter(n, tp_peers, others):
    barrier = pltpu.get_barrier_semaphore()
    for p in tp_peers:
        pl.semaphore_signal(barrier, inc=1, device_id={"tp": p}, device_id_type=pl.DeviceIdType.MESH)
    for o in others:
        pl.semaphore_signal(barrier, inc=1, device_id={"ctx": o}, device_id_type=pl.DeviceIdType.MESH)
    pl.semaphore_wait(barrier, len(tp_peers) + len(others))


def columns_to_rows(columns, tokens):
    lane = lax.broadcasted_iota(jnp.int32, (tokens, 128), 1)
    packed = jnp.zeros((tokens, 128), f32)
    for i, column in enumerate(columns):
        packed = jnp.where(lane == i, column, packed)
    return packed.T[:8]


def rows_to_columns(rows):
    return jnp.concatenate([rows, jnp.zeros((120, rows.shape[1]), f32)], axis=0).T


def front_kernel(
    n,
    q_ref,
    k_ref,
    v_ref,
    res_ref,
    ow_hbm,
    ag_ref,
    mg_ref,
    info_ref,
    gate_hbm,
    up_hbm,
    down_hbm,
    out_ref,
    mid_ref,
    all_info,
    rows_ref,
    gate_buf,
    up_buf,
    down_buf,
    hidden,
    k_all,
    v_all,
    ow,
    att,
    part_send,
    part_recv,
    far_send,
    far_recv,
    stat_recv,
    tok,
    ow_sem,
    gate_sem,
    up_sem,
    down_sem,
    kv_send,
    kv_recv,
    part_ss,
    part_rs,
    far_sem,
    stat_ss,
    stat_rs,
    tok_ss,
    tok_rs,
    tail=None,
):
    tokens, width = q_ref.shape
    half_rows = tokens // 2
    c, t, sib, far, diag, others = peers(n)
    weight_copy = pltpu.make_async_copy(ow_hbm, ow, ow_sem)
    weight_copy.start()
    tile = gate_buf.shape[2]
    steps = gate_hbm.shape[2] // tile
    ring = gate_buf.shape[0]
    halves = width // OUT_TILE
    block_order = (diag, sib, far, t)

    def wide_copies(i, slot):
        cols = pl.ds(pl.multiple_of(i * tile, 128), tile)
        return (
            pltpu.make_async_copy(gate_hbm.at[0, :, cols], gate_buf.at[slot], gate_sem.at[slot]),
            pltpu.make_async_copy(up_hbm.at[0, :, cols], up_buf.at[slot], up_sem.at[slot]),
        )

    def down_cols(block, h):
        return pl.ds(pl.multiple_of(block * width + h * OUT_TILE, 128), OUT_TILE)

    def down_copy(block, h):
        return pltpu.make_async_copy(
            down_hbm.at[0, :, down_cols(block, h)], down_buf.at[h], down_sem.at[h]
        )

    for i in range(ring):
        for copy in wide_copies(i, i):
            copy.start()
    for h in range(halves):
        down_copy(block_order[0], h).start()
    enter(n, (sib, far, diag), others)

    k_all[c] = k_ref[...]
    v_all[c] = v_ref[...]
    before = (
        lax.broadcasted_iota(jnp.int32, (tokens, tokens), 0)
        < lax.broadcasted_iota(jnp.int32, (tokens, tokens), 1)
    ).astype(f32).astype(bf16)
    info = info_ref[...]
    slots = jnp.dot(info.astype(bf16), before, preferred_element_type=f32)
    slots = jnp.where(info > 0.5, slots, -1.0)
    row = lax.broadcasted_iota(jnp.int32, info.shape, 0)
    all_info[c] = jnp.where(row == 0, slots, info)
    kv_copies = []
    for i, o in enumerate(others):
        for j, ref in enumerate((k_all, v_all, all_info)):
            copy = remote(ref.at[c], ref.at[c], kv_send.at[i, j], kv_recv.at[c, j], ctx=o)
            copy.start()
            kv_copies.append(copy)
    heads = range(width // HD)

    def score(h, keys):
        return lax.dot_general(
            q_ref[:, h * HD : (h + 1) * HD],
            keys,
            (((1,), (1,)), ((), ())),
            preferred_element_type=f32,
        ) * (1.0 / math.sqrt(HD))

    causal = lax.broadcasted_iota(jnp.int32, (tokens, tokens), 1) <= lax.broadcasted_iota(
        jnp.int32, (tokens, tokens), 0
    )
    own_keys, own_values = k_ref[...], v_ref[...]
    own_scores = [jnp.where(causal, score(h, own_keys), masked_score) for h in heads]
    own_max = [jnp.max(s, axis=1, keepdims=True) for s in own_scores]
    for o in others:
        for j, ref in enumerate((k_all, v_all, all_info)):
            remote(ref.at[o], ref.at[o], kv_send.at[0, j], kv_recv.at[o, j], ctx=o).wait_recv()

    for h in heads:
        scores = [own_scores[h]]
        row_max = own_max[h]
        for o in others:
            scores.append(jnp.where(o < c, score(h, k_all[o]), masked_score))
            row_max = jnp.maximum(row_max, jnp.max(scores[-1], axis=1, keepdims=True))
        total, weighted = 0.0, 0.0
        for part, values in zip(scores, [own_values] + [v_all[o] for o in others]):
            weights = jnp.exp(part - row_max)
            total = total + jnp.sum(weights, axis=1, keepdims=True)
            weighted = weighted + jnp.dot(
                weights.astype(bf16), values, preferred_element_type=f32
            )
        att[:, h * HD : (h + 1) * HD] = (weighted / total).astype(bf16)

    weight_copy.wait()

    def partial(block):
        cols = pl.ds(pl.multiple_of(block * width, 128), width)
        return jnp.dot(att[...], ow[:, cols], preferred_element_type=f32)

    sib_copies = []
    for j, block in enumerate((diag, sib)):
        part_send[j] = partial(block).astype(bf16)
        copy = remote(
            part_send.at[j], part_recv.at[j], part_ss.at[j], part_rs.at[j], tp=sib
        )
        copy.start()
        sib_copies.append(copy)
    keep = partial(far)
    sib_copies[0].wait()
    far_send[...] = (keep + part_recv[0].astype(f32)).astype(bf16)
    far_copy = remote(far_send, far_recv, far_sem.at[0], far_sem.at[1], tp=far)
    far_copy.start()
    own = partial(t)
    sib_copies[1].wait()
    own = own + part_recv[1].astype(f32)
    far_copy.wait()
    own = own + far_recv[...].astype(f32)

    residual = res_ref[...].astype(f32)
    gained = ag_ref[...][None, :] * own
    stat_recv[t] = columns_to_rows(
        [
            jnp.sum(own * own, axis=1, keepdims=True),
            jnp.sum(residual * residual, axis=1, keepdims=True),
            jnp.sum(residual * gained, axis=1, keepdims=True),
            jnp.sum(gained * gained, axis=1, keepdims=True),
        ],
        tokens,
    )
    stat_copies = []
    for i, p in enumerate((far, diag, sib)):
        copy = remote(stat_recv.at[t], stat_recv.at[t], stat_ss.at[i], stat_rs.at[t], tp=p)
        copy.start()
        stat_copies.append(copy)
    for i, p in enumerate((far, diag, sib)):
        remote(stat_recv.at[p], stat_recv.at[p], stat_ss.at[i], stat_rs.at[p], tp=p).wait_recv()
    sums = rows_to_columns(stat_recv[0] + stat_recv[1] + stat_recv[2] + stat_recv[3])
    scale = lax.rsqrt(sums[:, 0:1] / D + epsilon)
    squares = sums[:, 1:2] + 2.0 * scale * sums[:, 2:3] + scale * scale * sums[:, 3:4]
    middle = residual + gained * scale
    mid_ref[...] = middle
    tok[c, t] = (
        mg_ref[...][None, :] * middle * lax.rsqrt(jnp.maximum(squares, 0.0) / D + epsilon)
    ).astype(bf16)

    sent = []

    def piece(cb, tb, half):
        return tok.at[cb, tb, pl.ds(half * half_rows, half_rows)]

    def push(cb, tb, half, **where):
        ref = piece(cb, tb, half)
        copy = remote(ref, ref, tok_ss.at[len(sent)], tok_rs.at[cb, tb, half], **where)
        copy.start()
        sent.append(copy)

    def arrive(cb, tb, half):
        ref = piece(cb, tb, half)
        remote(ref, ref, tok_ss.at[0], tok_rs.at[cb, tb, half], tp=sib).wait_recv()

    for half in (0, 1):
        for o in others:
            push(c, t, half, ctx=o)
        push(c, t, 1 - half, tp=far)
    for half in (0, 1):
        push(c, t, half, tp=sib)
    for o in others:
        arrive(o, t, 0)
        push(o, t, 0, tp=far)
        push(o, t, 0, tp=sib)
    arrive(c, far, 1)
    for o in others:
        push(c, far, 1, ctx=o)
    push(c, far, 1, tp=sib)
    for o in others:
        arrive(o, t, 1)
        push(o, t, 1, tp=sib)
    arrive(c, far, 0)
    push(c, far, 0, tp=sib)
    for o in others:
        for half in (0, 1):
            arrive(o, far, half)
            push(o, far, half, tp=sib)
    for b in [c] + others:
        for block in (sib, diag):
            for half in (0, 1):
                arrive(b, block, half)
    gates = []
    for b in range(n):
        chosen = (
            lax.broadcasted_iota(jnp.int32, (CAP, tokens), 0).astype(f32) == all_info[b, 0:1, :]
        )
        gates.append(
            jnp.sum(jnp.where(chosen, all_info[b, 1:2, :], 0.0), axis=1, keepdims=True)
        )
        table = chosen.astype(f32).astype(bf16)
        for block in range(TP):
            rows_ref[b * CAP : (b + 1) * CAP, block * width : (block + 1) * width] = jnp.dot(
                table, tok[b, block], preferred_element_type=f32
            ).astype(bf16)
    row_gate = jnp.concatenate(gates, axis=0)

    @pl.loop(0, steps)
    def _(i):
        slot = i % ring
        for copy in wide_copies(i, slot):
            copy.wait()
        gate_part = jnp.dot(rows_ref[...], gate_buf[slot], preferred_element_type=f32)
        up_part = jnp.dot(rows_ref[...], up_buf[slot], preferred_element_type=f32)
        hidden[:, pl.ds(pl.multiple_of(i * tile, 128), tile)] = (
            gate_part / (1.0 + jnp.exp(-gate_part)) * up_part
        ).astype(bf16)

        @pl.when(i + ring < steps)
        def _():
            for copy in wide_copies(i + ring, slot):
                copy.start()

    stages = tail() if tail else iter(())
    next(stages, None)
    for at, block in enumerate(block_order):

        @pl.loop(0, halves)
        def _(h):
            down_copy(block, h).wait()
            portion = (
                jnp.dot(hidden[...], down_buf[h], preferred_element_type=f32) * row_gate
            ).astype(bf16)
            for b in range(n):
                out_ref[b, :, down_cols(block, h)] = portion[b * CAP : (b + 1) * CAP]
            if at + 1 < TP:
                down_copy(block_order[at + 1], h).start()

        next(stages, None)

    for copy in kv_copies + stat_copies + sent:
        copy.wait_send()


def front(n, fused, queries, key_rows, value_rows, residual, out_weight, ag, mg, info, gate, up, down, og):
    tokens, width = queries.shape
    units = gate.shape[2]
    tile, ring = (512, 3 if fused else 4) if units >= 4096 else (256, 1)
    halves = width // OUT_TILE
    vmem = pl.BlockSpec(memory_space=pltpu.VMEM)
    hbm = pl.BlockSpec(memory_space=pl.ANY)
    dma = pltpu.SemaphoreType.DMA
    pushes = 2 * (n - 1) + 2 + 2 + 2 * (n - 1) + (n - 1) + 1 + (n - 1) + 1 + 2 * (n - 1)
    inputs = [vmem] * 4 + [hbm] + [vmem] * 3 + [hbm] * 3
    made = (((n, CAP, D), bf16), ((tokens, width), f32), ((n, 8, tokens), f32))
    if fused:
        kernel = functools.partial(fused_kernel, n)
        outputs = jax.ShapeDtypeStruct((tokens, width), bf16)
        inputs.append(vmem)
        before = [pltpu.VMEM(*m) for m in made]
        after = back_scratch(n, tokens, width)
    else:
        kernel = functools.partial(front_kernel, n)
        outputs = tuple(jax.ShapeDtypeStruct(*m) for m in made)
        before = after = []
    return pl.pallas_call(
        kernel,
        out_shape=outputs,
        in_specs=inputs,
        out_specs=vmem if fused else (vmem,) * 3,
        scratch_shapes=before
        + [
            pltpu.VMEM((n * CAP, D), bf16),
            pltpu.VMEM((ring, D, tile), bf16),
            pltpu.VMEM((ring, D, tile), bf16),
            pltpu.VMEM((halves, units, OUT_TILE), bf16),
            pltpu.VMEM((n * CAP, units), bf16),
            pltpu.VMEM((n, tokens, HD), bf16),
            pltpu.VMEM((n, tokens, HD), bf16),
            pltpu.VMEM(out_weight.shape, bf16),
            pltpu.VMEM((tokens, width), bf16),
            pltpu.VMEM((2, tokens, width), bf16),
            pltpu.VMEM((2, tokens, width), bf16),
            pltpu.VMEM((tokens, width), bf16),
            pltpu.VMEM((tokens, width), bf16),
            pltpu.VMEM((TP, 8, tokens), f32),
            pltpu.VMEM((n, TP, tokens, width), bf16),
            dma,
            dma((ring,)),
            dma((ring,)),
            dma((halves,)),
            dma((max(n - 1, 1), 3)),
            dma((n, 3)),
            dma((2,)),
            dma((2,)),
            dma((2,)),
            dma((3,)),
            dma((TP,)),
            dma((pushes,)),
            dma((n, TP, 2)),
        ]
        + after,
        compiler_params=pltpu.CompilerParams(
            collective_id=0, has_side_effects=True, vmem_limit_bytes=VMEM_LIMIT
        ),
        name="front",
    )(queries, key_rows, value_rows, residual, out_weight, ag, mg, info, gate, up, down, *([og] if fused else []))


BACK_SCRATCH = 18


def back_scratch(n, tokens, width):
    dma = pltpu.SemaphoreType.DMA
    return [
        pltpu.VMEM((n, 2, tokens, width), bf16),
        pltpu.VMEM((n, 2, tokens, width), bf16),
        pltpu.VMEM((n, 2, tokens, width), f32),
        pltpu.VMEM((n, 2, tokens, width), bf16),
        pltpu.VMEM((n, tokens // 2, width), bf16),
        pltpu.VMEM((n, tokens // 2, width), bf16),
        pltpu.VMEM((tokens, width), bf16),
        pltpu.VMEM((n, tokens, width), bf16),
        pltpu.VMEM((TP, 8, tokens), f32),
        dma((n, 2)),
        dma((n, 2)),
        dma((n, 4)),
        dma((n,)),
        dma((n,)),
        dma((2,)),
        dma((n, 2)),
        dma((3,)),
        dma((TP,)),
    ]


def back_stages(
    n,
    por_ref,
    info_ref,
    mid_ref,
    og_ref,
    out_ref,
    one_send,
    one_recv,
    sums,
    two_send,
    turn_far,
    turn_ctx,
    from_far,
    from_ctx,
    stat_recv,
    one_ss,
    one_rs,
    two_ss,
    turn_far_rs,
    turn_ctx_rs,
    from_far_rs,
    from_ctx_rs,
    stat_ss,
    stat_rs,
):
    tokens, width = mid_ref.shape
    half_rows = tokens // 2
    first, second = pl.ds(0, half_rows), pl.ds(half_rows, half_rows)
    c, t, sib, far, diag, others = peers(n)

    def spread(b):
        slot = rows_to_columns(info_ref[b])[:, 0:1]
        return (
            lax.broadcasted_iota(jnp.int32, (tokens, CAP), 1).astype(f32) == slot
        ).astype(f32).astype(bf16)

    def partial(table, b, block):
        cols = pl.ds(pl.multiple_of(block * width, 128), width)
        return jnp.dot(table, por_ref[b, :, cols], preferred_element_type=f32)

    copies = []

    def push(src, dst, ss, rs, **where):
        copy = remote(src, dst, ss, rs, **where)
        copy.start()
        copies.append(copy)

    order = others + [c]
    tables = [spread(b) for b in order]
    for j, block in ((1, diag), (0, sib)):
        yield
        for i, b in enumerate(order):
            one_send[b, j] = partial(tables[i], b, block).astype(bf16)
            push(one_send.at[b, j], one_recv.at[b, j], one_ss.at[i, j], one_rs.at[b, j], tp=sib)
    for j, block in ((1, far), (0, t)):
        yield
        for i, b in enumerate(order):
            own = partial(tables[i], b, block)
            remote(
                one_send.at[b, j], one_recv.at[b, j], one_ss.at[i, j], one_rs.at[b, j], tp=sib
            ).wait_recv()
            own = own + one_recv[b, j].astype(f32)
            sums[b, j] = own
            if i < n - 1:
                two_send[b, j] = own.astype(bf16)
                if j == 1:
                    push(
                        two_send.at[b, 1, first],
                        turn_far.at[b],
                        two_ss.at[i, 0],
                        turn_far_rs.at[b],
                        tp=far,
                    )
                    push(
                        two_send.at[b, 1, second],
                        turn_ctx.at[c],
                        two_ss.at[i, 1],
                        turn_ctx_rs.at[c],
                        ctx=b,
                    )
                else:
                    push(
                        two_send.at[b, 0, second],
                        from_ctx.at[c, second],
                        two_ss.at[i, 2],
                        from_ctx_rs.at[c, 1],
                        ctx=b,
                    )
            elif j == 1:
                two_send[c, 1, first] = own[:half_rows].astype(bf16)
                push(
                    two_send.at[c, 1, first],
                    from_far.at[first],
                    two_ss.at[i, 0],
                    from_far_rs.at[0],
                    tp=far,
                )
    for i, b in enumerate(others):
        remote(
            two_send.at[b, 1, first], turn_far.at[b], two_ss.at[i, 0], turn_far_rs.at[b], tp=far
        ).wait_recv()
        two_send[b, 0, first] = (sums[b, 0, first] + turn_far[b].astype(f32)).astype(bf16)
        push(
            two_send.at[b, 0, first],
            from_ctx.at[c, first],
            two_ss.at[i, 3],
            from_ctx_rs.at[c, 0],
            ctx=b,
        )
    turned = sums[c, 1, second]
    for i, b in enumerate(others):
        remote(
            two_send.at[b, 1, second], turn_ctx.at[b], two_ss.at[i, 1], turn_ctx_rs.at[b], ctx=b
        ).wait_recv()
        turned = turned + turn_ctx[b].astype(f32)
    two_send[c, 1, second] = turned.astype(bf16)
    push(
        two_send.at[c, 1, second],
        from_far.at[second],
        two_ss.at[n - 1, 1],
        from_far_rs.at[1],
        tp=far,
    )
    mixture = sums[c, 0]
    for b in others:
        for half, rows in ((1, second), (0, first)):
            remote(
                two_send.at[b, 0, rows],
                from_ctx.at[b, rows],
                two_ss.at[0, 2],
                from_ctx_rs.at[b, half],
                ctx=b,
            ).wait_recv()
        mixture = mixture + from_ctx[b].astype(f32)
    for half, rows in ((0, first), (1, second)):
        remote(
            two_send.at[c, 1, rows],
            from_far.at[rows],
            two_ss.at[0, 0],
            from_far_rs.at[half],
            tp=far,
        ).wait_recv()
    mixture = mixture + from_far[...].astype(f32)

    stat_recv[t] = columns_to_rows(
        [jnp.sum(mixture * mixture, axis=1, keepdims=True)], tokens
    )
    for i, p in enumerate((far, diag, sib)):
        push(stat_recv.at[t], stat_recv.at[t], stat_ss.at[i], stat_rs.at[t], tp=p)
    for i, p in enumerate((far, diag, sib)):
        remote(stat_recv.at[p], stat_recv.at[p], stat_ss.at[i], stat_rs.at[p], tp=p).wait_recv()
    squares = rows_to_columns(stat_recv[0] + stat_recv[1] + stat_recv[2] + stat_recv[3])[:, 0:1]
    normed = og_ref[...][None, :] * mixture * lax.rsqrt(squares / D + epsilon)
    out_ref[...] = (mid_ref[...] + normed).astype(bf16)
    for copy in copies:
        copy.wait_send()


def back_kernel(n, *refs):
    c, t, sib, far, diag, others = peers(n)
    enter(n, (sib, far, diag), others)
    for _ in back_stages(n, *refs):
        pass


def fused_kernel(n, *refs):
    inputs, og_ref, out_ref = refs[:11], refs[11], refs[12]
    por_ref, mid_ref, all_info = refs[13:16]
    scratch = refs[16:-BACK_SCRATCH]

    def tail():
        return back_stages(
            n, por_ref, all_info, mid_ref, og_ref, out_ref, *refs[-BACK_SCRATCH:]
        )

    front_kernel(n, *inputs, por_ref, mid_ref, all_info, *scratch, tail=tail)


def back(n, portions, info, middle, og):
    tokens, width = middle.shape
    vmem = pl.BlockSpec(memory_space=pltpu.VMEM)
    return pl.pallas_call(
        functools.partial(back_kernel, n),
        out_shape=jax.ShapeDtypeStruct((tokens, width), bf16),
        in_specs=[vmem] * 4,
        out_specs=vmem,
        scratch_shapes=back_scratch(n, tokens, width),
        compiler_params=pltpu.CompilerParams(
            collective_id=1, has_side_effects=True, vmem_limit_bytes=VMEM_LIMIT
        ),
        name="back",
    )(portions, info, middle, og)


def shards(
    n,
    queries,
    key_rows,
    value_rows,
    residual,
    out_weight,
    attention_gain,
    middle_gain,
    output_gain,
    gate_weight,
    up_weight,
    down_weight,
    routes,
    gate_shares,
):
    tokens = queries.shape[0]
    mine = routes == lax.axis_index("tp")
    named = jnp.sum(mine.astype(f32), axis=1)
    gate = jnp.sum(jnp.where(mine, gate_shares, 0.0), axis=1)
    row = jnp.arange(8, dtype=jnp.int32)[:, None]
    info = jnp.where(row == 0, named[None, :], jnp.where(row == 1, gate[None, :], 0.0))
    fused = n == 2
    result = front(
        n,
        fused,
        queries,
        key_rows,
        value_rows,
        residual,
        out_weight,
        attention_gain,
        middle_gain,
        info,
        gate_weight,
        up_weight,
        down_weight,
        output_gain,
    )
    if fused:
        return result
    portions, middle, info = result
    return back(n, portions, info, middle, output_gain)


def solution(mesh):
    in_specs = (
        P(("dp", "ctx"), "tp"),
        P(("dp", "ctx"), "tp"),
        P(("dp", "ctx"), "tp"),
        P(("dp", "ctx"), "tp"),
        P("tp", None),
        P("tp"),
        P("tp"),
        P("tp"),
        P("tp", None, "ctx"),
        P("tp", None, "ctx"),
        P("tp", "ctx", None),
        P(("dp", "ctx"), None),
        P(("dp", "ctx"), None),
    )
    out_specs = P(("dp", "ctx"), "tp")
    return jax.shard_map(
        functools.partial(shards, mesh.shape["ctx"]),
        mesh=mesh,
        in_specs=in_specs,
        out_specs=out_specs,
        check_vma=False,
    )
```
